32 devices in a mesh: req: 4 (over z), seq: 8 (over y, x, core).
Axes of the slice: x: 2, y: 2, z: 4, core: 2. Of those that a mesh axis runs over, the one named last changes fastest.
Arguments:
- tokens: bfloat16 [4, 8, 512, 1024], P('req', 'seq'), may hold values from -6 to 6
- norm_gain: float32 [1024], replicated, may hold values from 0.5 to 1.5
- w_qkv: bfloat16 [1024, 3072], replicated, may hold values from -0.1875 to 0.1875
- w_out: bfloat16 [1024, 1024], replicated, may hold values from -0.1875 to 0.1875
- w_gates: bfloat16 [1024, 24], replicated, may hold values from -0.1875 to 0.1875
- gate_bias: float32 [3, 8], replicated, may hold values from -3 to 3
- persistent: bfloat16 [2, 16, 1024], replicated, may hold values from -8 to 8
- cache: bfloat16 [4, 8, 8, 2, 32, 1024], P('req', 'seq'), may hold values from -60 to 60
- page_back: int32 [4, 8, 8], P('req', 'seq'), may hold values from 0 to 5, as said below
- page_fill: int32 [4, 8, 8], P('req', 'seq'), may hold values from 1 to 32
- mem_state: float32 [4, 8, 8, 128, 128], P('req', 'seq'), may hold values from -2 to 2
- mig_source: int32 [8, 4], P('seq'), may hold values from 0 to 3, each once within a row
Outputs:
- output: bfloat16 [4, 8, 512, 1024], P('req', 'seq')
The draws below stay inside these ranges and needn't reach their ends.
Inputs may be any that keep to these rules, and one draw needn't show every extreme that they name: `page_back`: on every cycle position no value occurs more than 2 times among its pages; cycle position 0 of every group has pages with value 5. `mig_source`: every row is a permutation of the groups.
All inputs are finite; a program needn't handle non-finite values.
Results may differ from the reference program's by a relative error of at most 0.008.
Values may be sent and summed in bfloat16 or wider, within the bound.
No kernel may reach another device: no remote copies, remote signals or barrier semaphores. Data moves between devices by JAX's collectives and lax.ppermute only.
A program may use at most 128 MiB of HBM per device.

```python
import jax
import jax.numpy as jnp
from jax import lax

D = 1024
HEADS = 8
HEAD_DIM = 128
PERS = 16
BLK = 64
STRETCH = 512
PAGE = 32
PAGES_DEV = 8
SPAN = 6
GROUPS = 4
SLOTS = 8


def draw_cache(key, part):
    key_main = jax.random.fold_in(key, 0)
    shape = (GROUPS, SLOTS, PAGES_DEV, 2, PAGE, HEADS * HEAD_DIM)
    values = jnp.clip(jax.random.normal(key_main, shape, jnp.float32), -6.0, 6.0)
    return values.astype(jnp.bfloat16)


def draw_page_back(key, part):
    key_heavy, key_jitter, key_coin = jax.random.split(key, 3)
    heavy = (jax.random.randint(key_heavy, (GROUPS, SLOTS), 0, 4) == 0).astype(jnp.int32)
    offsets = jnp.arange(SPAN, dtype=jnp.int32)
    owners = (jnp.arange(SLOTS, dtype=jnp.int32)[:, None] - offsets[None, :]) % SLOTS
    heavy_near = heavy[:, owners]
    jitter = jax.random.randint(key_jitter, (GROUPS, SLOTS, SPAN), 0, 65536)
    forced = ((jnp.arange(SLOTS, dtype=jnp.int32)[:, None] == 0) & (offsets[None, :] == SPAN - 1)).astype(jnp.int32)
    scores = (jitter + heavy_near * 131072 + forced[None] * 524288) * SPAN + offsets[None, None, :]
    ranked = lax.top_k(scores, PAGES_DEV // 2 + 1)[1].astype(jnp.int32)
    split_coin = jax.random.randint(key_coin, (GROUPS, SLOTS, 1), 0, 2)
    page_index = jnp.arange(PAGES_DEV, dtype=jnp.int32)
    last_page = (page_index == PAGES_DEV - 1).astype(jnp.int32)
    page_rank = page_index[None, None, :] // 2 + last_page[None, None, :] * split_coin
    return jnp.take_along_axis(ranked, page_rank, axis=2).astype(jnp.int32)


def place_ends(result, stream_key, smallest, top_value):
    longest = result.shape.index(max(result.shape))
    spots = []
    for shift in (0, 1):
        where = [jax.random.randint(jax.random.fold_in(stream_key, axis), (), 0, length) for axis, length in enumerate(result.shape)]
        where[longest] = (where[longest] + shift) % result.shape[longest]
        spots.append(tuple(where))
    return result.at[spots[0]].set(smallest).at[spots[1]].set(top_value)


def levels(stream_key, shape, pieces, least, high):
    gain = 1.0
    for dim, shards_of in pieces:
        steps = jax.random.uniform(jax.random.fold_in(jax.random.fold_in(stream_key, 6), dim), (shards_of,), jnp.float32, least / len(pieces), high / len(pieces))
        gain = gain * jnp.repeat(jnp.exp(steps), shape[dim] // shards_of).reshape((-1,) + (1,) * (len(shape) - 1 - dim))
    return gain


def scatter_about(own_key, shape, scale, most, pieces=(), kind=jnp.bfloat16):
    factor_of = levels(own_key, shape, pieces, -0.22, 0.18) if pieces else 1.0
    array = jax.random.normal(own_key, shape, jnp.float32) * scale * factor_of
    return jnp.minimum(jnp.maximum(array, -most), most).astype(kind)


def setup_inputs(seed: int = 0) -> dict:
    seeds = jax.random.split(jax.random.key(seed), 13)
    tokens = scatter_about(seeds[0], (GROUPS, SLOTS, STRETCH, D), 1.0, 6.0, ((0, 4), (1, 8)))
    norm_gain = jnp.clip(1.0 + 0.1 * jax.random.normal(seeds[1], (D,), jnp.float32), 0.5, 1.5)
    w_qkv = scatter_about(seeds[2], (D, 3 * HEADS * HEAD_DIM), D ** -0.5, 0.1875)
    w_out = scatter_about(seeds[3], (HEADS * HEAD_DIM, D), (HEADS * HEAD_DIM) ** -0.5, 0.1875)
    w_gates = scatter_about(seeds[4], (D, 3 * HEADS), D ** -0.5, 0.1875)
    gate_bias = jnp.clip(jax.random.uniform(seeds[5], (3, HEADS), jnp.float32, -3.0, 3.0), -3.0, 3.0)
    persistent = scatter_about(seeds[6], (2, PERS, HEADS * HEAD_DIM), 1.5, 8.0)
    cache = draw_cache(jax.random.fold_in(seeds[12], 71), 0)
    page_back = draw_page_back(jax.random.fold_in(seeds[12], 71), 0)
    page_fill = place_ends(jax.random.randint(seeds[9], (GROUPS, SLOTS, PAGES_DEV), 1, PAGE + 1), jax.random.fold_in(seeds[9], 1), 1, PAGE).astype(jnp.int32)
    mem_state = scatter_about(seeds[10], (GROUPS, SLOTS, HEADS, HEAD_DIM, HEAD_DIM), 0.3, 2.0, ((0, 4), (1, 8)), jnp.float32)
    mig_source = jax.vmap(lambda own: jax.random.permutation(own, GROUPS))(jax.random.split(seeds[11], SLOTS)).reshape((SLOTS, GROUPS)).astype(jnp.int32)
    return {"tokens": tokens, "norm_gain": norm_gain, "w_qkv": w_qkv, "w_out": w_out, "w_gates": w_gates, "gate_bias": gate_bias, "persistent": persistent, "cache": cache, "page_back": page_back, "page_fill": page_fill, "mem_state": mem_state, "mig_source": mig_source}


masked_score = -1e+30

def unit_rows(matrix):
    return matrix * lax.rsqrt(lax.optimization_barrier(jnp.sum(matrix * matrix, axis=-1, keepdims=True)) + 1e-06)

def memory_reads(projected, gate_pre, gate_bias, state):
    length = projected.shape[0]
    blocks = length // BLK
    width = HEADS * HEAD_DIM

    def heads_first(columns):
        return jnp.transpose(columns.astype(jnp.float32).reshape(blocks, BLK, HEADS, HEAD_DIM), (0, 2, 1, 3))
    queries = unit_rows(heads_first(projected[:, :width]))
    keys = unit_rows(heads_first(projected[:, width:2 * width]))
    values = heads_first(projected[:, 2 * width:])
    block_mean = lax.optimization_barrier(jnp.mean(gate_pre.reshape(blocks, BLK, 3 * HEADS), axis=1))
    decay = jnp.exp(-jax.nn.softplus(block_mean[:, :HEADS] + gate_bias[0] - 2.5))
    rate = 0.5 * jax.nn.sigmoid(block_mean[:, HEADS:2 * HEADS] + gate_bias[1])

    def advance(memory, inputs):
        query_block, key_block, value_block, decay_now, rate_now = inputs
        read = jnp.einsum('hij,htj->hti', memory, query_block, precision=lax.Precision.HIGHEST)
        error = jnp.einsum('hij,htj->hti', memory, key_block, precision=lax.Precision.HIGHEST) - value_block
        gradient = jnp.einsum('hti,htj->hij', error, key_block, precision=lax.Precision.HIGHEST)
        memory = decay_now[:, None, None] * memory - rate_now[:, None, None] * gradient
        return (memory, read)
    last_state, reads = lax.scan(advance, state, (queries, keys, values, decay, rate))
    return jnp.transpose(reads, (0, 2, 1, 3)).reshape(length, HEADS, HEAD_DIM)

def process(inputs, blocks, backs, fills, state, norm_gain, w_qkv, w_out, w_gates, gate_bias, persistent):
    length = inputs.shape[0]
    width = HEADS * HEAD_DIM
    rows = inputs.astype(jnp.float32)
    normed = (rows * lax.rsqrt(lax.optimization_barrier(jnp.mean(rows * rows, axis=-1, keepdims=True)) + 1e-05) * norm_gain).astype(jnp.bfloat16)
    projected = lax.optimization_barrier(jnp.dot(normed, w_qkv, preferred_element_type=jnp.float32).astype(jnp.bfloat16))
    gate_pre = jnp.dot(normed, w_gates, preferred_element_type=jnp.float32)
    cached = blocks.reshape(SPAN * PAGES_DEV, 2, PAGE, width)
    all_keys = jnp.concatenate([persistent[0], cached[:, 0].reshape(-1, width), projected[:, width:2 * width]], axis=0)
    all_values = jnp.concatenate([persistent[1], cached[:, 1].reshape(-1, width), projected[:, 2 * width:]], axis=0)
    offsets = jnp.arange(SPAN, dtype=jnp.int32)
    inside = jnp.arange(PAGE, dtype=jnp.int32)[None, None, :] < fills[:, :, None]
    cache_visible = ((backs == offsets[:, None])[:, :, None] & inside).reshape(1, -1)
    position = jnp.arange(length, dtype=jnp.int32)
    visible = jnp.concatenate([jnp.ones((length, PERS), dtype=jnp.bool_), jnp.broadcast_to(cache_visible, (length, cache_visible.shape[1])), position[:, None] >= position[None, :]], axis=1)
    queries = projected[:, :width].astype(jnp.float32).reshape(length, HEADS, HEAD_DIM)
    key_heads = all_keys.astype(jnp.float32).reshape(-1, HEADS, HEAD_DIM)
    value_heads = all_values.astype(jnp.float32).reshape(-1, HEADS, HEAD_DIM)
    scores = jnp.einsum('thd,shd->hts', queries, key_heads) * HEAD_DIM ** (-0.5)
    scores = jnp.where(visible[None], scores, masked_score)
    weights = jnp.exp(scores - lax.optimization_barrier(jnp.max(scores, axis=2, keepdims=True)))
    total = lax.optimization_barrier(jnp.sum(weights, axis=2))
    rounded = lax.optimization_barrier(weights.astype(jnp.bfloat16)).astype(jnp.float32)
    attended = jnp.einsum('hts,shd->thd', rounded, value_heads) / jnp.transpose(total)[:, :, None]
    reads = memory_reads(projected, gate_pre, gate_bias, state)
    mix = jax.nn.sigmoid(gate_pre[:, 2 * HEADS:] + gate_bias[2])
    combined = (attended + mix[:, :, None] * reads).reshape(length, width).astype(jnp.bfloat16)
    return jnp.dot(combined, w_out, preferred_element_type=jnp.float32).astype(jnp.bfloat16)

def reference(tokens, norm_gain, w_qkv, w_out, w_gates, gate_bias, persistent, cache, page_back, page_fill, mem_state, mig_source):
    slot_index = jnp.arange(SLOTS, dtype=jnp.int32)
    source = jnp.transpose(mig_source).astype(jnp.int32)
    moved_cache = cache[source, slot_index[None, :]]
    moved_back = page_back[source, slot_index[None, :]]
    moved_fill = page_fill[source, slot_index[None, :]]
    moved_state = mem_state[source, slot_index[None, :]]

    def one_request(flat):
        group = flat // SLOTS
        place = flat % SLOTS
        cycle = ((place + jnp.arange(SPAN, dtype=jnp.int32)) % SLOTS).astype(jnp.int32)
        blocks = moved_cache[group, cycle]
        backs = moved_back[group, cycle]
        fills = moved_fill[group, cycle]
        return process(tokens[group, place], blocks, backs, fills, moved_state[group, place], norm_gain, w_qkv, w_out, w_gates, gate_bias, persistent)
    results = lax.map(one_request, jnp.arange(GROUPS * SLOTS, dtype=jnp.int32))
    return results.reshape(GROUPS, SLOTS, STRETCH, D)
```

```python
import itertools

import jax
import jax.numpy as jnp
from jax import lax
from jax.experimental import pallas as pl
from jax.experimental.pallas import tpu as pltpu
from jax.sharding import PartitionSpec as P

HEADS = 8
HEAD_DIM = 128
BLK = 64
SPAN = 6
CAPK = 2
LOG2E = 1.4426950408889634
SCALE2 = HEAD_DIM ** (-0.5) * LOG2E
MASKED = -1e30
MARK = 128.0
TILE = 16
VMEM = pl.BlockSpec(memory_space=pltpu.VMEM)
SMEM = pl.BlockSpec(memory_space=pltpu.SMEM)


def nt(a, b):
    return lax.dot_general(a, b, (((1,), (1,)), ((), ())), preferred_element_type=jnp.float32)


def nn(a, b):
    return lax.dot_general(a, b, (((1,), (0,)), ((), ())), preferred_element_type=jnp.float32)


def params(mib):
    return pltpu.CompilerParams(vmem_limit_bytes=mib * 1024 * 1024)


def project_kernel(tokens_ref, gain_ref, w_ref, wg_ref, out_ref, gates_ref, normed_ref):
    @pl.when(pl.program_id(0) == 0)
    def _():
        rows = tokens_ref[...].astype(jnp.float32)
        mean = jnp.mean(rows * rows, axis=-1, keepdims=True)
        normed_ref[...] = (rows * lax.rsqrt(mean + 1e-05) * gain_ref[...]).astype(jnp.bfloat16)
        gates_ref[...] = nn(normed_ref[...], wg_ref[...])

    out_ref[...] = nn(normed_ref[...], w_ref[...]).astype(jnp.bfloat16)


def project(tokens, gain, w_qkv, w_gates):
    length, width = tokens.shape
    columns = w_qkv.shape[1]
    tile = 512
    return pl.pallas_call(
        project_kernel,
        grid=(columns // tile,),
        in_specs=[
            pl.BlockSpec((length, width), lambda i: (0, 0)),
            pl.BlockSpec((1, width), lambda i: (0, 0)),
            pl.BlockSpec((width, tile), lambda i: (0, i)),
            pl.BlockSpec(w_gates.shape, lambda i: (0, 0)),
        ],
        out_specs=[
            pl.BlockSpec((length, tile), lambda i: (0, i)),
            pl.BlockSpec((length, w_gates.shape[1]), lambda i: (0, 0)),
        ],
        out_shape=[
            jax.ShapeDtypeStruct((length, columns), jnp.bfloat16),
            jax.ShapeDtypeStruct((length, w_gates.shape[1]), jnp.float32),
        ],
        scratch_shapes=[pltpu.VMEM((length, width), jnp.bfloat16)],
        compiler_params=params(24),
        cost_estimate=pl.CostEstimate(
            flops=2 * length * width * columns,
            bytes_accessed=2 * (width * columns + length * width + length * columns),
            transcendentals=0,
        ),
        name="project",
    )(tokens, gain.reshape(1, width), w_qkv, w_gates)


def own_kernel(proj_ref, lasting_ref, sum_ref, top_ref, total_ref):
    length = proj_ref.shape[0]
    width = HEADS * HEAD_DIM
    half = length // 2
    lasting = lasting_ref.shape[1]
    tops, totals = [], []
    for h in range(HEADS):
        cols = slice(h * HEAD_DIM, (h + 1) * HEAD_DIM)
        kcols = slice(width + h * HEAD_DIM, width + (h + 1) * HEAD_DIM)
        vcols = slice(2 * width + h * HEAD_DIM, 2 * width + (h + 1) * HEAD_DIM)
        pkeys = lasting_ref[0, :, cols]
        pvalues = lasting_ref[1, :, cols]
        head_top, head_total = [], []
        for part in range(2):
            rows = slice(part * half, (part + 1) * half)
            upto = (part + 1) * half
            q = proj_ref[rows, cols]
            s0 = nt(q, pkeys)
            s1 = nt(q, proj_ref[0:upto, kcols])
            qi = lax.broadcasted_iota(jnp.int32, (half, upto), 0) + part * half
            ki = lax.broadcasted_iota(jnp.int32, (half, upto), 1)
            s1 = jnp.where(qi >= ki, s1, MASKED)
            top = jnp.maximum(
                jnp.max(s0, axis=1, keepdims=True), jnp.max(s1, axis=1, keepdims=True)
            )
            p0 = jnp.exp2((s0 - top) * SCALE2)
            p1 = jnp.exp2((s1 - top) * SCALE2)
            total = jnp.sum(p0, axis=1, keepdims=True) + jnp.sum(p1, axis=1, keepdims=True)
            sum_ref[rows, cols] = nn(p0.astype(jnp.bfloat16), pvalues) + nn(
                p1.astype(jnp.bfloat16), proj_ref[0:upto, vcols]
            )
            head_top.append(top)
            head_total.append(total)
        tops.append(jnp.concatenate(head_top, axis=0))
        totals.append(jnp.concatenate(head_total, axis=0))
    top_ref[...] = jnp.concatenate(tops, axis=1)
    total_ref[...] = jnp.concatenate(totals, axis=1)


def own_attention(projected, persistent):
    length = projected.shape[0]
    width = HEADS * HEAD_DIM
    return pl.pallas_call(
        own_kernel,
        in_specs=[VMEM, VMEM],
        out_specs=[VMEM, VMEM, VMEM],
        out_shape=[
            jax.ShapeDtypeStruct((length, width), jnp.float32),
            jax.ShapeDtypeStruct((length, HEADS), jnp.float32),
            jax.ShapeDtypeStruct((length, HEADS), jnp.float32),
        ],
        compiler_params=params(32),
        cost_estimate=pl.CostEstimate(
            flops=3 * length * length * width,
            bytes_accessed=10 * length * width,
            transcendentals=length * length * HEADS,
        ),
        name="own",
    )(projected, persistent)


def memory_kernel(proj_ref, gates_ref, bias_ref, state_ref, out_ref, mem_ref):
    length = proj_ref.shape[0]
    width = HEADS * HEAD_DIM
    blocks = length // BLK
    for h in range(HEADS):
        mem_ref[h] = state_ref[:, h * HEAD_DIM : (h + 1) * HEAD_DIM].astype(jnp.float32)
    means = jnp.concatenate(
        [jnp.mean(gates_ref[b * BLK : (b + 1) * BLK, :], axis=0, keepdims=True) for b in range(blocks)],
        axis=0,
    )
    decay = 1.0 / (1.0 + jnp.exp(means[:, :HEADS] + bias_ref[0:1, :] - 2.5))
    rate = 0.5 / (1.0 + jnp.exp(-(means[:, HEADS : 2 * HEADS] + bias_ref[1:2, :])))
    mix = 1.0 / (1.0 + jnp.exp(-(gates_ref[:, 2 * HEADS :] + bias_ref[2:3, :])))
    for b in range(blocks):
        rows = slice(b * BLK, (b + 1) * BLK)
        for h in range(HEADS):
            cols = slice(h * HEAD_DIM, (h + 1) * HEAD_DIM)
            q = proj_ref[rows, cols]
            k = proj_ref[rows, slice(width + h * HEAD_DIM, width + (h + 1) * HEAD_DIM)]
            v = proj_ref[rows, slice(2 * width + h * HEAD_DIM, 2 * width + (h + 1) * HEAD_DIM)]
            qf, kf = q.astype(jnp.float32), k.astype(jnp.float32)
            unit_q = lax.rsqrt(jnp.sum(qf * qf, axis=1, keepdims=True) + 1e-06)
            unit_k = lax.rsqrt(jnp.sum(kf * kf, axis=1, keepdims=True) + 1e-06)
            mem = mem_ref[h]
            both = nn(jnp.concatenate([q, k], axis=0), mem.astype(jnp.bfloat16))
            out_ref[rows, cols] = both[:BLK] * (unit_q * mix[rows, h : h + 1])
            if b < blocks - 1:
                error = both[BLK:] * unit_k - v.astype(jnp.float32)
                step = error * (unit_k * -rate[b : b + 1, h : h + 1])
                mem_ref[h] = mem * decay[b : b + 1, h : h + 1] + nn(
                    jnp.transpose(kf).astype(jnp.bfloat16), step.astype(jnp.bfloat16)
                )


def memory_reads(projected, gates, gate_bias, moved, cached):
    length = projected.shape[0]
    width = HEADS * HEAD_DIM
    state_spec = pl.BlockSpec((HEAD_DIM, width), lambda i: (cached // HEAD_DIM, 0))
    return pl.pallas_call(
        memory_kernel,
        grid=(1,),
        in_specs=[VMEM] * 3 + [state_spec],
        out_specs=VMEM,
        out_shape=jax.ShapeDtypeStruct((length, width), jnp.float32),
        scratch_shapes=[pltpu.VMEM((HEADS, HEAD_DIM, HEAD_DIM), jnp.float32)],
        compiler_params=params(32),
        cost_estimate=pl.CostEstimate(
            flops=6 * length * HEAD_DIM * width,
            bytes_accessed=10 * length * width,
            transcendentals=0,
        ),
        name="memory",
    )(projected, gates, gate_bias, moved)


def prepare_kernel(sources_ref, back_ref, fill_ref, state_ref, cache_ref, out_ref, code_ref, rows_ref, sem):
    cached = cache_ref.shape[0]
    pages = back_ref.shape[2]
    groups = sources_ref.shape[1]
    whole = pltpu.make_async_copy(cache_ref, out_ref.at[pl.ds(0, cached)], sem.at[0])
    whole.start()
    code = jnp.int32(0)
    for g in range(groups - 1):
        smaller = jnp.int32(0)
        for later in range(g + 1, groups):
            smaller = smaller + (sources_ref[0, later] < sources_ref[0, g]).astype(jnp.int32)
        code = code * (groups - g) + smaller
    code_ref[0] = code
    for h in range(HEADS):
        cols = slice(h * HEAD_DIM, (h + 1) * HEAD_DIM)
        rows_ref[0:HEAD_DIM, cols] = jnp.transpose(state_ref[h]).astype(jnp.bfloat16)
    lane = lax.broadcasted_iota(jnp.int32, (TILE, HEAD_DIM), 1)
    line = jnp.zeros((TILE, HEAD_DIM), jnp.float32)
    for page in range(pages):
        line = jnp.where(lane == page, back_ref[0, 0, page].astype(jnp.float32), line)
        line = jnp.where(lane == pages + page, fill_ref[0, 0, page].astype(jnp.float32), line)
    rows_ref[HEAD_DIM:, :] = jnp.zeros((TILE, rows_ref.shape[1]), jnp.bfloat16)
    rows_ref[HEAD_DIM:, 0:HEAD_DIM] = line.astype(jnp.bfloat16)
    rest = pltpu.make_async_copy(rows_ref, out_ref.at[pl.ds(cached, HEAD_DIM + TILE)], sem.at[1])
    rest.start()
    whole.wait()
    rest.wait()


def prepare(sources, back, fill, state, cache):
    cached, width = cache.shape
    return pl.pallas_call(
        prepare_kernel,
        in_specs=[SMEM, SMEM, SMEM, VMEM, pl.BlockSpec(memory_space=pl.ANY)],
        out_specs=[pl.BlockSpec(memory_space=pl.ANY), SMEM],
        out_shape=[
            jax.ShapeDtypeStruct((cached + HEAD_DIM + TILE, width), cache.dtype),
            jax.ShapeDtypeStruct((1,), jnp.int32),
        ],
        scratch_shapes=[
            pltpu.VMEM((HEAD_DIM + TILE, width), cache.dtype),
            pltpu.SemaphoreType.DMA((2,)),
        ],
        compiler_params=params(16),
        cost_estimate=pl.CostEstimate(flops=0, bytes_accessed=3 * 1024 * 1024, transcendentals=0),
        name="prepare",
    )(sources, back, fill, state, cache)


def pack_kernel(table_ref, moved_ref, *rest):
    outs, (where_ref, fill_ref) = rest[:SPAN], rest[SPAN:]
    page_rows = outs[0].shape[1] * outs[0].shape[2]
    page_len = outs[0].shape[2]
    pages = moved_ref.shape[0] // page_rows
    for slot in range(SPAN * CAPK):
        where_ref[slot] = 0
        fill_ref[slot] = 0
    for page in range(pages):
        first = table_ref[page] * CAPK
        slot = first + jnp.where(fill_ref[first] > 0, 1, 0)
        where_ref[slot] = page
        fill_ref[slot] = table_ref[pages + page]
    row = lax.broadcasted_iota(jnp.int32, (page_len, HEAD_DIM), 0)
    for distance in range(SPAN):
        for j in range(CAPK):
            start = pl.multiple_of(where_ref[distance * CAPK + j] * page_rows, page_rows)
            fill = fill_ref[distance * CAPK + j]
            keys = moved_ref[pl.ds(start, page_len), :]
            outs[distance][j, 0] = keys
            outs[distance][j, 1] = moved_ref[pl.ds(start + page_len, page_len), :]
            marked = jnp.where(
                (row == page_len - 1) & (fill < page_len),
                MARK + fill.astype(jnp.float32),
                keys[:, 0:HEAD_DIM].astype(jnp.float32),
            )
            outs[distance][j, 0, :, 0:HEAD_DIM] = marked.astype(jnp.bfloat16)


def pack_pages(table, moved, page_shape, cached):
    width = moved.shape[1]
    shape = (CAPK,) + page_shape
    return pl.pallas_call(
        pack_kernel,
        grid=(1,),
        in_specs=[SMEM, pl.BlockSpec((cached, width), lambda i: (0, 0))],
        out_specs=[VMEM] * SPAN,
        out_shape=[jax.ShapeDtypeStruct(shape, moved.dtype)] * SPAN,
        scratch_shapes=[pltpu.SMEM((SPAN * CAPK,), jnp.int32)] * 2,
        compiler_params=params(16),
        cost_estimate=pl.CostEstimate(flops=0, bytes_accessed=3 * 1024 * 1024, transcendentals=0),
        name="pack",
    )(table, moved)


def finish_kernel(proj_ref, sum_ref, top_ref, total_ref, read_ref, w_ref, *rest):
    pages = rest[:SPAN]
    out_ref, combined_ref = rest[SPAN:]
    length = sum_ref.shape[0]
    page_len = pages[0].shape[2]
    slots = SPAN * CAPK
    lane = lax.broadcasted_iota(jnp.int32, (1, page_len), 1).astype(jnp.float32)
    visible = []
    for distance in range(SPAN):
        for j in range(CAPK):
            flag = pages[distance][j, 0, :, 0:HEAD_DIM].astype(jnp.float32)[
                page_len - 1 : page_len, 0:1
            ]
            fill = jnp.where(flag > MARK - 1.0, flag - MARK, float(page_len))
            visible.append(lane < fill)
    hide = jnp.concatenate([jnp.where(seen, 0.0, MASKED) for seen in visible], axis=1)
    for h in range(HEADS):
        cols = slice(h * HEAD_DIM, (h + 1) * HEAD_DIM)
        q = proj_ref[:, cols]
        keys = jnp.concatenate(
            [pages[d][j, 0, :, cols] for d in range(SPAN) for j in range(CAPK)], axis=0
        )
        values = jnp.concatenate(
            [pages[d][j, 1, :, cols] for d in range(SPAN) for j in range(CAPK)], axis=0
        )
        s = nt(q, keys) + hide
        before = top_ref[:, h : h + 1]
        top = jnp.maximum(before, jnp.max(s, axis=1, keepdims=True))
        p = jnp.exp2((s - top) * SCALE2)
        shrink = jnp.exp2((before - top) * SCALE2)
        total = total_ref[:, h : h + 1] * shrink + jnp.sum(p, axis=1, keepdims=True)
        gathered = sum_ref[:, cols] * shrink + nn(p.astype(jnp.bfloat16), values)
        combined_ref[:, cols] = (gathered / total + read_ref[:, cols]).astype(jnp.bfloat16)
    out_ref[...] = nn(combined_ref[...], w_ref[...]).astype(jnp.bfloat16)


def finish(projected, own_sum, top, total, reads, w_out, pages):
    length, width = own_sum.shape
    return pl.pallas_call(
        finish_kernel,
        grid=(1,),
        in_specs=[pl.BlockSpec((length, width), lambda i: (0, 0))] + [VMEM] * (5 + SPAN),
        out_specs=VMEM,
        out_shape=jax.ShapeDtypeStruct((length, w_out.shape[1]), jnp.bfloat16),
        scratch_shapes=[pltpu.VMEM((length, width), jnp.bfloat16)],
        compiler_params=params(40),
        cost_estimate=pl.CostEstimate(
            flops=2 * length * width * (w_out.shape[1] + 768),
            bytes_accessed=16 * length * width,
            transcendentals=length * 384 * HEADS,
        ),
        name="finish",
    )(projected, own_sum, top, total, reads, w_out, *pages)


def shifted(block, axis, distance):
    size = lax.axis_size(axis)
    return lax.ppermute(block, axis, [((i - distance) % size, i) for i in range(size)])


def migrate(code, payload):
    groups = lax.axis_size("req")
    orders = list(itertools.permutations(range(groups)))

    def branch(order):
        route = [(order[g], g) for g in range(groups)]
        return lambda x: lax.ppermute(x, "req", route)

    return lax.switch(code, [branch(order) for order in orders], payload)


def on_device(
    tokens,
    norm_gain,
    w_qkv,
    w_out,
    w_gates,
    gate_bias,
    persistent,
    cache,
    page_back,
    page_fill,
    mem_state,
    mig_source,
):
    pages = cache.shape[2]
    rows = cache.reshape(-1, cache.shape[-1])
    cached = rows.shape[0]
    payload, code = prepare(mig_source, page_back, page_fill, mem_state[0, 0], rows)
    moved = migrate(code[0], payload)
    table = moved[-1, : 2 * pages].astype(jnp.int32)
    packed = pack_pages(table, moved, cache.shape[3:], cached)
    arrived = [packed[0]] + [shifted(packed[k], "seq", -k) for k in range(1, SPAN)]
    projected, gates = project(tokens[0, 0], norm_gain, w_qkv, w_gates)
    own_sum, top, total = own_attention(projected, persistent)
    reads = memory_reads(projected, gates, gate_bias, moved, cached)
    result = finish(projected, own_sum, top, total, reads, w_out, arrived)
    return result[None, None]


def solution(mesh):
    return jax.shard_map(
        on_device,
        mesh=mesh,
        in_specs=(
            P("req", "seq", None, None),
            P(),
            P(),
            P(),
            P(),
            P(),
            P(),
            P("req", "seq", None, None, None, None),
            P("req", "seq", None),
            P("req", "seq", None),
            P("req", "seq", None, None, None),
            P("seq", None),
        ),
        out_specs=P("req", "seq", None, None),
        check_vma=False,
    )
```

```python
import itertools

import jax
import jax.numpy as jnp
from jax import lax
from jax.experimental import pallas as pl
from jax.experimental.pallas import tpu as pltpu
from jax.sharding import PartitionSpec as P

HEADS = 8
HEAD_DIM = 128
BLK = 64
SPAN = 6
CAPK = 2
LOG2E = 1.4426950408889634
SCALE2 = HEAD_DIM ** (-0.5) * LOG2E
MASKED = -1e30
MARK = 128.0
TILE = 16
VMEM = pl.BlockSpec(memory_space=pltpu.VMEM)
SMEM = pl.BlockSpec(memory_space=pltpu.SMEM)
ANY = pl.BlockSpec(memory_space=pl.ANY)


def nt(a, b):
    return lax.dot_general(a, b, (((1,), (1,)), ((), ())), preferred_element_type=jnp.float32)


def nn(a, b):
    return lax.dot_general(a, b, (((1,), (0,)), ((), ())), preferred_element_type=jnp.float32)


def params(mib):
    return pltpu.CompilerParams(vmem_limit_bytes=mib * 1024 * 1024)


def project_kernel(tokens_ref, gain_ref, w_ref, wg_ref, out_ref, gates_ref, normed_ref):
    @pl.when(pl.program_id(0) == 0)
    def _():
        rows = tokens_ref[...].astype(jnp.float32)
        mean = jnp.mean(rows * rows, axis=-1, keepdims=True)
        normed_ref[...] = (rows * lax.rsqrt(mean + 1e-05) * gain_ref[...]).astype(jnp.bfloat16)
        gates_ref[...] = nn(normed_ref[...], wg_ref[...])

    out_ref[...] = nn(normed_ref[...], w_ref[...]).astype(jnp.bfloat16)


def project(tokens, gain, w_qkv, w_gates):
    length, width = tokens.shape
    columns = w_qkv.shape[1]
    tile = 512
    return pl.pallas_call(
        project_kernel,
        grid=(columns // tile,),
        in_specs=[
            pl.BlockSpec((length, width), lambda i: (0, 0)),
            pl.BlockSpec((1, width), lambda i: (0, 0)),
            pl.BlockSpec((width, tile), lambda i: (0, i)),
            pl.BlockSpec(w_gates.shape, lambda i: (0, 0)),
        ],
        out_specs=[
            pl.BlockSpec((length, tile), lambda i: (0, i)),
            pl.BlockSpec((length, w_gates.shape[1]), lambda i: (0, 0)),
        ],
        out_shape=[
            jax.ShapeDtypeStruct((length, columns), jnp.bfloat16),
            jax.ShapeDtypeStruct((length, w_gates.shape[1]), jnp.float32),
        ],
        scratch_shapes=[pltpu.VMEM((length, width), jnp.bfloat16)],
        compiler_params=params(24),
        cost_estimate=pl.CostEstimate(
            flops=2 * length * width * columns,
            bytes_accessed=2 * (width * columns + length * width + length * columns),
            transcendentals=0,
        ),
        name="project",
    )(tokens, gain.reshape(1, width), w_qkv, w_gates)


def own_kernel(proj_ref, lasting_ref, sum_ref, top_ref, total_ref):
    length = proj_ref.shape[0]
    width = HEADS * HEAD_DIM
    half = length // 2
    key = lax.broadcasted_iota(jnp.int32, (half, half), 0)
    token = lax.broadcasted_iota(jnp.int32, (half, half), 1)
    causal = key <= token
    for h in range(HEADS):
        cols = slice(h * HEAD_DIM, (h + 1) * HEAD_DIM)
        keys = proj_ref[:, width + h * HEAD_DIM : width + (h + 1) * HEAD_DIM]
        values = jnp.concatenate(
            [
                lasting_ref[1, :, cols],
                proj_ref[:, 2 * width + h * HEAD_DIM : 2 * width + (h + 1) * HEAD_DIM],
            ],
            axis=0,
        )
        turned = jnp.transpose(values)
        for part in range(2):
            rows = slice(part * half, (part + 1) * half)
            q = proj_ref[rows, cols]
            scores = [nt(lasting_ref[0, :, cols], q)]
            scores += [nt(keys[i * half : (i + 1) * half], q) for i in range(part)]
            scores.append(jnp.where(causal, nt(keys[rows], q), MASKED))
            top = scores[0].max(axis=0, keepdims=True)
            for s in scores[1:]:
                top = jnp.maximum(top, s.max(axis=0, keepdims=True))
            shift = top * SCALE2
            weights = [jnp.exp2(s * SCALE2 - shift) for s in scores]
            total = weights[0].sum(axis=0, keepdims=True)
            for w in weights[1:]:
                total = total + w.sum(axis=0, keepdims=True)
            rounded = jnp.concatenate([w.astype(jnp.bfloat16) for w in weights], axis=0)
            sum_ref[cols, rows] = nn(turned[:, : rounded.shape[0]], rounded)
            top_ref[h : h + 1, rows] = top
            total_ref[h : h + 1, rows] = total


def own_attention(projected, persistent):
    length = projected.shape[0]
    width = HEADS * HEAD_DIM
    return pl.pallas_call(
        own_kernel,
        in_specs=[VMEM, VMEM],
        out_specs=[VMEM, VMEM, VMEM],
        out_shape=[
            jax.ShapeDtypeStruct((width, length), jnp.float32),
            jax.ShapeDtypeStruct((HEADS, length), jnp.float32),
            jax.ShapeDtypeStruct((HEADS, length), jnp.float32),
        ],
        compiler_params=params(32),
        cost_estimate=pl.CostEstimate(
            flops=3 * length * length * width,
            bytes_accessed=10 * length * width,
            transcendentals=length * length * HEADS,
        ),
        name="own",
    )(projected, persistent)


def memory_kernel(proj_ref, gates_ref, bias_ref, state_ref, out_ref, mem_ref):
    length = proj_ref.shape[0]
    width = HEADS * HEAD_DIM
    blocks = length // BLK
    for h in range(HEADS):
        mem_ref[h] = state_ref[:, h * HEAD_DIM : (h + 1) * HEAD_DIM].astype(jnp.float32)
    means = jnp.concatenate(
        [jnp.mean(gates_ref[b * BLK : (b + 1) * BLK, :], axis=0, keepdims=True) for b in range(blocks)],
        axis=0,
    )
    decay = 1.0 / (1.0 + jnp.exp(means[:, :HEADS] + bias_ref[0:1, :] - 2.5))
    rate = 0.5 / (1.0 + jnp.exp(-(means[:, HEADS : 2 * HEADS] + bias_ref[1:2, :])))
    mix = 1.0 / (1.0 + jnp.exp(-(gates_ref[:, 2 * HEADS :] + bias_ref[2:3, :])))
    for b in range(blocks):
        rows = slice(b * BLK, (b + 1) * BLK)
        for h in range(HEADS):
            cols = slice(h * HEAD_DIM, (h + 1) * HEAD_DIM)
            q = proj_ref[rows, cols]
            k = proj_ref[rows, slice(width + h * HEAD_DIM, width + (h + 1) * HEAD_DIM)]
            v = proj_ref[rows, slice(2 * width + h * HEAD_DIM, 2 * width + (h + 1) * HEAD_DIM)]
            qf, kf = q.astype(jnp.float32), k.astype(jnp.float32)
            unit_q = lax.rsqrt(jnp.sum(qf * qf, axis=1, keepdims=True) + 1e-06)
            unit_k = lax.rsqrt(jnp.sum(kf * kf, axis=1, keepdims=True) + 1e-06)
            mem = mem_ref[h]
            both = nn(jnp.concatenate([q, k], axis=0), mem.astype(jnp.bfloat16))
            out_ref[rows, cols] = both[:BLK] * (unit_q * mix[rows, h : h + 1])
            if b < blocks - 1:
                error = both[BLK:] * unit_k - v.astype(jnp.float32)
                step = error * (unit_k * -rate[b : b + 1, h : h + 1])
                mem_ref[h] = mem * decay[b : b + 1, h : h + 1] + nn(
                    jnp.transpose(kf).astype(jnp.bfloat16), step.astype(jnp.bfloat16)
                )


def memory_reads(projected, gates, gate_bias, moved, cached):
    length = projected.shape[0]
    width = HEADS * HEAD_DIM
    state_spec = pl.BlockSpec((HEAD_DIM, width), lambda i: (cached // HEAD_DIM, 0))
    return pl.pallas_call(
        memory_kernel,
        grid=(1,),
        in_specs=[VMEM] * 3 + [state_spec],
        out_specs=VMEM,
        out_shape=jax.ShapeDtypeStruct((length, width), jnp.float32),
        scratch_shapes=[pltpu.VMEM((HEADS, HEAD_DIM, HEAD_DIM), jnp.float32)],
        compiler_params=params(32),
        cost_estimate=pl.CostEstimate(
            flops=6 * length * HEAD_DIM * width,
            bytes_accessed=10 * length * width,
            transcendentals=0,
        ),
        name="memory",
    )(projected, gates, gate_bias, moved)


def prepare_kernel(
    sources_ref, back_ref, fill_ref, state_ref, cache_ref, out_ref, code_ref,
    order_ref, place_ref, used_ref, held_ref, rows_ref, sem,
):
    cached = cache_ref.shape[0]
    pages = back_ref.shape[2]
    groups = sources_ref.shape[1]
    loads = [
        pltpu.make_async_copy(sources_ref, order_ref, sem.at[0]),
        pltpu.make_async_copy(back_ref.at[0], place_ref, sem.at[1]),
        pltpu.make_async_copy(fill_ref.at[0], used_ref, sem.at[2]),
        pltpu.make_async_copy(state_ref, held_ref, sem.at[3]),
    ]
    for load in loads:
        load.start()
    whole = pltpu.make_async_copy(cache_ref, out_ref.at[pl.ds(0, cached)], sem.at[4])
    whole.start()
    for load in loads:
        load.wait()
    code = jnp.int32(0)
    for g in range(groups - 1):
        smaller = jnp.int32(0)
        for later in range(g + 1, groups):
            smaller = smaller + (order_ref[0, later] < order_ref[0, g]).astype(jnp.int32)
        code = code * (groups - g) + smaller
    code_ref[0] = code
    lane = lax.broadcasted_iota(jnp.int32, (TILE, HEAD_DIM), 1)
    line = jnp.zeros((TILE, HEAD_DIM), jnp.float32)
    for page in range(pages):
        line = jnp.where(lane == page, place_ref[0, page].astype(jnp.float32), line)
        line = jnp.where(lane == pages + page, used_ref[0, page].astype(jnp.float32), line)
    rows_ref[HEAD_DIM:, :] = jnp.zeros((TILE, rows_ref.shape[1]), jnp.bfloat16)
    rows_ref[HEAD_DIM:, 0:HEAD_DIM] = line.astype(jnp.bfloat16)
    for h in range(HEADS):
        cols = slice(h * HEAD_DIM, (h + 1) * HEAD_DIM)
        rows_ref[0:HEAD_DIM, cols] = jnp.transpose(held_ref[h]).astype(jnp.bfloat16)
    rest = pltpu.make_async_copy(rows_ref, out_ref.at[pl.ds(cached, HEAD_DIM + TILE)], sem.at[5])
    rest.start()
    whole.wait()
    rest.wait()


def prepare(sources, back, fill, state, cache):
    cached, width = cache.shape
    pages = back.shape[2]
    return pl.pallas_call(
        prepare_kernel,
        in_specs=[ANY] * 5,
        out_specs=[ANY, SMEM],
        out_shape=[
            jax.ShapeDtypeStruct((cached + HEAD_DIM + TILE, width), cache.dtype),
            jax.ShapeDtypeStruct((1,), jnp.int32),
        ],
        scratch_shapes=[
            pltpu.SMEM(sources.shape, jnp.int32),
            pltpu.SMEM((1, pages), jnp.int32),
            pltpu.SMEM((1, pages), jnp.int32),
            pltpu.VMEM(state.shape, state.dtype),
            pltpu.VMEM((HEAD_DIM + TILE, width), cache.dtype),
            pltpu.SemaphoreType.DMA((6,)),
        ],
        compiler_params=params(56),
        cost_estimate=pl.CostEstimate(flops=0, bytes_accessed=3 * 1024 * 1024, transcendentals=0),
        name="prepare",
    )(sources, back, fill, state, cache)


def pack_kernel(moved_ref, *rest):
    outs = rest[:SPAN]
    held_ref, line_ref, where_ref, count_ref, sem = rest[SPAN:]
    page_len = outs[0].shape[2]
    page_rows = outs[0].shape[1] * page_len
    pages = held_ref.shape[0] - 1
    cached = pages * page_rows
    table = pltpu.make_async_copy(
        moved_ref.at[pl.ds(moved_ref.shape[0] - TILE, TILE), pl.ds(0, HEAD_DIM)], line_ref, sem.at[0]
    )
    table.start()
    loads = [
        pltpu.make_async_copy(
            moved_ref.at[pl.ds(page * page_rows + half * page_len, page_len)],
            held_ref.at[page, half],
            sem.at[1 + 2 * page + half],
        )
        for page in range(pages)
        for half in range(2)
    ]
    for load in loads:
        load.start()
    row = lax.broadcasted_iota(jnp.int32, (TILE, HEAD_DIM), 0)
    held_ref[pages] = jnp.zeros(held_ref.shape[1:], held_ref.dtype)
    held_ref[pages, 0, page_len - TILE :, 0:HEAD_DIM] = jnp.full(
        (TILE, HEAD_DIM), MARK, held_ref.dtype
    )
    for slot in range(SPAN * CAPK):
        where_ref[slot] = pages
    for distance in range(SPAN):
        count_ref[distance] = 0
    table.wait()
    line = line_ref[...].astype(jnp.float32)
    lane = lax.broadcasted_iota(jnp.int32, (TILE, HEAD_DIM), 1)
    top = row == 0
    entries = [
        jnp.sum(jnp.where(top & (lane == i), line, 0.0)).astype(jnp.int32) for i in range(2 * pages)
    ]
    for page in range(pages):
        distance = entries[page]
        taken = count_ref[distance]
        where_ref[distance * CAPK + taken] = page
        count_ref[distance] = taken + 1
    for page in range(pages):
        loads[2 * page].wait()
        loads[2 * page + 1].wait()
        fill = entries[pages + page]
        tile = held_ref[page, 0, page_len - TILE :, 0:HEAD_DIM]
        marked = jnp.where(
            (row == TILE - 1) & (fill < page_len), MARK + fill.astype(jnp.float32), tile.astype(jnp.float32)
        )
        held_ref[page, 0, page_len - TILE :, 0:HEAD_DIM] = marked.astype(held_ref.dtype)
    stores = [
        pltpu.make_async_copy(
            held_ref.at[where_ref[distance * CAPK + j]],
            outs[distance].at[j],
            sem.at[1 + 2 * pages + distance * CAPK + j],
        )
        for distance in range(SPAN)
        for j in range(CAPK)
    ]
    for store in stores:
        store.start()
    for store in stores:
        store.wait()


def pack_pages(moved, pages, page_shape):
    shape = (CAPK,) + page_shape
    return pl.pallas_call(
        pack_kernel,
        in_specs=[ANY],
        out_specs=[ANY] * SPAN,
        out_shape=[jax.ShapeDtypeStruct(shape, moved.dtype)] * SPAN,
        scratch_shapes=[
            pltpu.VMEM((pages + 1,) + page_shape, moved.dtype),
            pltpu.VMEM((TILE, HEAD_DIM), moved.dtype),
            pltpu.SMEM((SPAN * CAPK,), jnp.int32),
            pltpu.SMEM((SPAN,), jnp.int32),
            pltpu.SemaphoreType.DMA((1 + 2 * pages + SPAN * CAPK,)),
        ],
        compiler_params=params(16),
        cost_estimate=pl.CostEstimate(flops=0, bytes_accessed=3 * 1024 * 1024, transcendentals=0),
        name="pack",
    )(moved)


def finish_kernel(proj_ref, sum_ref, top_ref, total_ref, read_ref, w_ref, *rest):
    pages = rest[:SPAN]
    out_ref, combined_ref = rest[SPAN:]
    page_len = pages[0].shape[2]
    row = lax.broadcasted_iota(jnp.int32, (page_len, HEAD_DIM), 0).astype(jnp.float32)
    hide = []
    for distance in range(SPAN):
        for j in range(CAPK):
            flag = pages[distance][j, 0, :, 0:HEAD_DIM].astype(jnp.float32)[
                page_len - 1 : page_len, 0:1
            ]
            fill = jnp.where(flag > MARK - 1.0, flag - MARK, float(page_len))
            hide.append(jnp.where(row < fill, 0.0, MASKED))
    hide = jnp.concatenate(hide, axis=0)[:, 0:1]
    for h in range(HEADS):
        cols = slice(h * HEAD_DIM, (h + 1) * HEAD_DIM)
        keys = jnp.concatenate(
            [pages[d][j, 0, :, cols] for d in range(SPAN) for j in range(CAPK)], axis=0
        )
        values = jnp.concatenate(
            [pages[d][j, 1, :, cols] for d in range(SPAN) for j in range(CAPK)], axis=0
        )
        s = nt(keys, proj_ref[:, cols]) + hide
        before = top_ref[h : h + 1, :]
        top = jnp.maximum(before, s.max(axis=0, keepdims=True))
        p = jnp.exp2(s * SCALE2 - top * SCALE2)
        shrink = jnp.exp2((before - top) * SCALE2)
        total = total_ref[h : h + 1, :] * shrink + p.sum(axis=0, keepdims=True)
        gathered = sum_ref[cols, :] * shrink + nn(jnp.transpose(values), p.astype(jnp.bfloat16))
        attended = jnp.transpose(gathered * (1.0 / total))
        combined_ref[:, cols] = (attended + read_ref[:, cols]).astype(jnp.bfloat16)
    out_ref[...] = nn(combined_ref[...], w_ref[...]).astype(jnp.bfloat16)


def finish(projected, own_sum, top, total, reads, w_out, pages):
    width, length = own_sum.shape
    return pl.pallas_call(
        finish_kernel,
        grid=(1,),
        in_specs=[pl.BlockSpec((length, width), lambda i: (0, 0))] + [VMEM] * (5 + SPAN),
        out_specs=VMEM,
        out_shape=jax.ShapeDtypeStruct((length, w_out.shape[1]), jnp.bfloat16),
        scratch_shapes=[pltpu.VMEM((length, width), jnp.bfloat16)],
        compiler_params=params(40),
        cost_estimate=pl.CostEstimate(
            flops=2 * length * width * (w_out.shape[1] + 768),
            bytes_accessed=16 * length * width,
            transcendentals=length * 384 * HEADS,
        ),
        name="finish",
    )(projected, own_sum, top, total, reads, w_out, *pages)


def shifted(block, axis, distance):
    size = lax.axis_size(axis)
    return lax.ppermute(block, axis, [((i - distance) % size, i) for i in range(size)])


def migrate(code, payload):
    groups = lax.axis_size("req")
    orders = list(itertools.permutations(range(groups)))

    def branch(order):
        route = [(order[g], g) for g in range(groups)]
        return lambda x: lax.ppermute(x, "req", route)

    return lax.switch(code, [branch(order) for order in orders], payload)


def on_device(
    tokens,
    norm_gain,
    w_qkv,
    w_out,
    w_gates,
    gate_bias,
    persistent,
    cache,
    page_back,
    page_fill,
    mem_state,
    mig_source,
):
    pages = cache.shape[2]
    rows = cache.reshape(-1, cache.shape[-1])
    cached = rows.shape[0]
    payload, code = prepare(mig_source, page_back, page_fill, mem_state[0, 0], rows)
    moved = migrate(code[0], payload)
    packed = pack_pages(moved, pages, cache.shape[3:])
    arrived = [packed[0]] + [shifted(packed[k], "seq", -k) for k in range(1, SPAN)]
    projected, gates = project(tokens[0, 0], norm_gain, w_qkv, w_gates)
    own_sum, top, total = own_attention(projected, persistent)
    reads = memory_reads(projected, gates, gate_bias, moved, cached)
    result = finish(projected, own_sum, top, total, reads, w_out, arrived)
    return result[None, None]


def solution(mesh):
    return jax.shard_map(
        on_device,
        mesh=mesh,
        in_specs=(
            P("req", "seq", None, None),
            P(),
            P(),
            P(),
            P(),
            P(),
            P(),
            P("req", "seq", None, None, None, None),
            P("req", "seq", None),
            P("req", "seq", None),
            P("req", "seq", None, None, None),
            P("seq", None),
        ),
        out_specs=P("req", "seq", None, None),
        check_vma=False,
    )
```

```python
import itertools

import jax
import jax.numpy as jnp
from jax import lax
from jax.experimental import pallas as pl
from jax.experimental.pallas import tpu as pltpu
from jax.sharding import PartitionSpec as P

HEADS = 8
HEAD_DIM = 128
BLK = 64
SPAN = 6
CAPK = 2
LOG2E = 1.4426950408889634
SCALE2 = HEAD_DIM ** (-0.5) * LOG2E
MASKED = -1e30
MARK = 128.0
TILE = 16
CHUNK = 128
VMEM = pl.BlockSpec(memory_space=pltpu.VMEM)
SMEM = pl.BlockSpec(memory_space=pltpu.SMEM)
ANY = pl.BlockSpec(memory_space=pl.ANY)


def nt(a, b):
    return lax.dot_general(a, b, (((1,), (1,)), ((), ())), preferred_element_type=jnp.float32)


def nn(a, b):
    return lax.dot_general(a, b, (((1,), (0,)), ((), ())), preferred_element_type=jnp.float32)


def params(mib):
    return pltpu.CompilerParams(vmem_limit_bytes=mib * 1024 * 1024)


def project_kernel(tokens_ref, gain_ref, w_ref, wg_ref, out_ref, gates_ref, normed_ref):
    length = tokens_ref.shape[0]

    def chunk(i):
        return pl.ds(pl.multiple_of(i * CHUNK, CHUNK), CHUNK)

    @pl.when(pl.program_id(0) == 0)
    def _():
        @pl.loop(0, length // CHUNK)
        def _(i):
            rows = tokens_ref[chunk(i), :].astype(jnp.float32)
            mean = jnp.mean(rows * rows, axis=-1, keepdims=True)
            normed = (rows * lax.rsqrt(mean + 1e-05) * gain_ref[...]).astype(jnp.bfloat16)
            normed_ref[chunk(i), :] = normed
            gates_ref[chunk(i), :] = nn(normed, wg_ref[...])

    @pl.loop(0, length // CHUNK)
    def _(i):
        out_ref[chunk(i), :] = nn(normed_ref[chunk(i), :], w_ref[...]).astype(jnp.bfloat16)


def project(tokens, gain, w_qkv, w_gates):
    length, width = tokens.shape
    columns = w_qkv.shape[1]
    tile = 512
    return pl.pallas_call(
        project_kernel,
        grid=(columns // tile,),
        in_specs=[
            pl.BlockSpec((length, width), lambda i: (0, 0)),
            pl.BlockSpec((1, width), lambda i: (0, 0)),
            pl.BlockSpec((width, tile), lambda i: (0, i)),
            pl.BlockSpec(w_gates.shape, lambda i: (0, 0)),
        ],
        out_specs=[
            pl.BlockSpec((length, tile), lambda i: (0, i)),
            pl.BlockSpec((length, w_gates.shape[1]), lambda i: (0, 0)),
        ],
        out_shape=[
            jax.ShapeDtypeStruct((length, columns), jnp.bfloat16),
            jax.ShapeDtypeStruct((length, w_gates.shape[1]), jnp.float32),
        ],
        scratch_shapes=[pltpu.VMEM((length, width), jnp.bfloat16)],
        compiler_params=params(24),
        cost_estimate=pl.CostEstimate(
            flops=2 * length * width * columns,
            bytes_accessed=2 * (width * columns + length * width + length * columns),
            transcendentals=0,
        ),
        name="project",
    )(tokens, gain.reshape(1, width), w_qkv, w_gates)


def own_kernel(proj_ref, lasting_ref, sum_ref, top_ref, total_ref):
    length = proj_ref.shape[0]
    width = HEADS * HEAD_DIM
    half = length // 2
    key = lax.broadcasted_iota(jnp.int32, (half, half), 0)
    token = lax.broadcasted_iota(jnp.int32, (half, half), 1)
    causal = key <= token
    for h in range(HEADS):
        cols = slice(h * HEAD_DIM, (h + 1) * HEAD_DIM)
        keys = proj_ref[:, width + h * HEAD_DIM : width + (h + 1) * HEAD_DIM]
        values = jnp.concatenate(
            [
                lasting_ref[1, :, cols],
                proj_ref[:, 2 * width + h * HEAD_DIM : 2 * width + (h + 1) * HEAD_DIM],
            ],
            axis=0,
        )
        turned = jnp.transpose(values)
        for part in range(2):
            rows = slice(part * half, (part + 1) * half)
            q = proj_ref[rows, cols]
            scores = [nt(lasting_ref[0, :, cols], q)]
            scores += [nt(keys[i * half : (i + 1) * half], q) for i in range(part)]
            scores.append(jnp.where(causal, nt(keys[rows], q), MASKED))
            top = scores[0].max(axis=0, keepdims=True)
            for s in scores[1:]:
                top = jnp.maximum(top, s.max(axis=0, keepdims=True))
            shift = top * SCALE2
            weights = [jnp.exp2(s * SCALE2 - shift) for s in scores]
            total = weights[0].sum(axis=0, keepdims=True)
            for w in weights[1:]:
                total = total + w.sum(axis=0, keepdims=True)
            rounded = jnp.concatenate([w.astype(jnp.bfloat16) for w in weights], axis=0)
            sum_ref[cols, rows] = nn(turned[:, : rounded.shape[0]], rounded)
            top_ref[h : h + 1, rows] = top
            total_ref[h : h + 1, rows] = total


def own_attention(projected, persistent):
    length = projected.shape[0]
    width = HEADS * HEAD_DIM
    return pl.pallas_call(
        own_kernel,
        in_specs=[VMEM, VMEM],
        out_specs=[VMEM, VMEM, VMEM],
        out_shape=[
            jax.ShapeDtypeStruct((width, length), jnp.float32),
            jax.ShapeDtypeStruct((HEADS, length), jnp.float32),
            jax.ShapeDtypeStruct((HEADS, length), jnp.float32),
        ],
        compiler_params=params(32),
        cost_estimate=pl.CostEstimate(
            flops=3 * length * length * width,
            bytes_accessed=10 * length * width,
            transcendentals=length * length * HEADS,
        ),
        name="own",
    )(projected, persistent)


def memory_kernel(proj_ref, gates_ref, bias_ref, out_ref, lead_ref, mem_ref):
    length = proj_ref.shape[0]
    width = HEADS * HEAD_DIM
    blocks = length // BLK
    means = jnp.concatenate(
        [jnp.mean(gates_ref[b * BLK : (b + 1) * BLK, :], axis=0, keepdims=True) for b in range(blocks)],
        axis=0,
    )
    decay = 1.0 / (1.0 + jnp.exp(means[:, :HEADS] + bias_ref[0:1, :] - 2.5))
    rate = 0.5 / (1.0 + jnp.exp(-(means[:, HEADS : 2 * HEADS] + bias_ref[1:2, :])))
    mix = 1.0 / (1.0 + jnp.exp(-(gates_ref[:, 2 * HEADS :] + bias_ref[2:3, :])))
    one = lax.broadcasted_iota(jnp.int32, (HEAD_DIM, HEAD_DIM), 0) == lax.broadcasted_iota(
        jnp.int32, (HEAD_DIM, HEAD_DIM), 1
    )
    for b in range(blocks):
        rows = slice(b * BLK, (b + 1) * BLK)
        for h in range(HEADS):
            cols = slice(h * HEAD_DIM, (h + 1) * HEAD_DIM)
            q = proj_ref[rows, cols]
            k = proj_ref[rows, slice(width + h * HEAD_DIM, width + (h + 1) * HEAD_DIM)]
            v = proj_ref[rows, slice(2 * width + h * HEAD_DIM, 2 * width + (h + 1) * HEAD_DIM)]
            qf, kf = q.astype(jnp.float32), k.astype(jnp.float32)
            unit_q = lax.rsqrt(jnp.sum(qf * qf, axis=1, keepdims=True) + 1e-06) * mix[rows, h : h + 1]
            unit_k = lax.rsqrt(jnp.sum(kf * kf, axis=1, keepdims=True) + 1e-06)
            fade = decay[b : b + 1, h : h + 1]
            if b == 0:
                out_ref[rows, cols] = jnp.zeros((BLK, HEAD_DIM), jnp.float32)
                lead_ref[rows, cols] = (qf * unit_q).astype(jnp.bfloat16)
                held = kf * unit_k
                kept = jnp.concatenate(
                    [jnp.zeros((HEAD_DIM, HEAD_DIM), jnp.float32), jnp.where(one, fade, 0.0)], axis=1
                )
                error = jnp.concatenate([-v.astype(jnp.float32), held], axis=1)
            else:
                mem = mem_ref[h]
                both = nn(jnp.concatenate([q, k], axis=0), mem.astype(jnp.bfloat16))
                out_ref[rows, cols] = both[:BLK, :HEAD_DIM] * unit_q
                lead_ref[rows, cols] = (both[:BLK, HEAD_DIM:] * unit_q).astype(jnp.bfloat16)
                if b == blocks - 1:
                    continue
                kept = mem * fade
                error = jnp.concatenate(
                    [
                        both[BLK:, :HEAD_DIM] * unit_k - v.astype(jnp.float32),
                        both[BLK:, HEAD_DIM:] * unit_k,
                    ],
                    axis=1,
                )
            step = error * (unit_k * -rate[b : b + 1, h : h + 1])
            mem_ref[h] = kept + nn(jnp.transpose(kf).astype(jnp.bfloat16), step.astype(jnp.bfloat16))


def memory_reads(projected, gates, gate_bias):
    length = projected.shape[0]
    width = HEADS * HEAD_DIM
    return pl.pallas_call(
        memory_kernel,
        in_specs=[VMEM] * 3,
        out_specs=[VMEM] * 2,
        out_shape=[
            jax.ShapeDtypeStruct((length, width), jnp.float32),
            jax.ShapeDtypeStruct((length, width), jnp.bfloat16),
        ],
        scratch_shapes=[pltpu.VMEM((HEADS, HEAD_DIM, 2 * HEAD_DIM), jnp.float32)],
        compiler_params=params(32),
        cost_estimate=pl.CostEstimate(
            flops=12 * length * HEAD_DIM * width,
            bytes_accessed=12 * length * width,
            transcendentals=0,
        ),
        name="memory",
    )(projected, gates, gate_bias)


def prepare_kernel(
    sources_ref, back_ref, fill_ref, cache_ref, out_ref, code_ref, away_ref,
    order_ref, place_ref, used_ref, rows_ref, sem,
):
    cached = cache_ref.shape[0]
    pages = back_ref.shape[2]
    groups = sources_ref.shape[1]
    loads = [
        pltpu.make_async_copy(sources_ref, order_ref, sem.at[0]),
        pltpu.make_async_copy(back_ref.at[0], place_ref, sem.at[1]),
        pltpu.make_async_copy(fill_ref.at[0], used_ref, sem.at[2]),
    ]
    for load in loads:
        load.start()
    whole = pltpu.make_async_copy(cache_ref, out_ref.at[pl.ds(0, cached)], sem.at[3])
    whole.start()
    for load in loads:
        load.wait()
    code = jnp.int32(0)
    for g in range(groups - 1):
        smaller = jnp.int32(0)
        for later in range(g + 1, groups):
            smaller = smaller + (order_ref[0, later] < order_ref[0, g]).astype(jnp.int32)
        code = code * (groups - g) + smaller
    code_ref[0] = code
    here = lax.axis_index("req")
    source, near = order_ref[0, here], here ^ 1
    away_ref[0] = jnp.where(source == here, 0, jnp.where(source == near, 1, 2))
    away_ref[1] = (order_ref[0, here ^ 2] == near).astype(jnp.int32)
    lane = lax.broadcasted_iota(jnp.int32, (TILE, HEAD_DIM), 1)
    line = jnp.zeros((TILE, HEAD_DIM), jnp.float32)
    for page in range(pages):
        line = jnp.where(lane == page, place_ref[0, page].astype(jnp.float32), line)
        line = jnp.where(lane == pages + page, used_ref[0, page].astype(jnp.float32), line)
    rows_ref[...] = jnp.zeros(rows_ref.shape, jnp.bfloat16)
    rows_ref[:, 0:HEAD_DIM] = line.astype(jnp.bfloat16)
    rest = pltpu.make_async_copy(rows_ref, out_ref.at[pl.ds(cached, TILE)], sem.at[4])
    rest.start()
    whole.wait()
    rest.wait()


def prepare(sources, back, fill, cache):
    cached, width = cache.shape
    pages = back.shape[2]
    return pl.pallas_call(
        prepare_kernel,
        in_specs=[ANY] * 4,
        out_specs=[ANY, SMEM, SMEM],
        out_shape=[
            jax.ShapeDtypeStruct((cached + TILE, width), cache.dtype),
            jax.ShapeDtypeStruct((1,), jnp.int32),
            jax.ShapeDtypeStruct((2,), jnp.int32),
        ],
        scratch_shapes=[
            pltpu.SMEM(sources.shape, jnp.int32),
            pltpu.SMEM((1, pages), jnp.int32),
            pltpu.SMEM((1, pages), jnp.int32),
            pltpu.VMEM((TILE, width), cache.dtype),
            pltpu.SemaphoreType.DMA((5,)),
        ],
        compiler_params=params(56),
        cost_estimate=pl.CostEstimate(flops=0, bytes_accessed=2 * 1024 * 1024, transcendentals=0),
        name="prepare",
    )(sources, back, fill, cache)


def pack_kernel(moved_ref, *rest):
    outs = rest[:SPAN]
    held_ref, line_ref, where_ref, count_ref, sem = rest[SPAN:]
    page_len = outs[0].shape[2]
    page_rows = outs[0].shape[1] * page_len
    pages = held_ref.shape[0] - 1
    cached = pages * page_rows
    table = pltpu.make_async_copy(
        moved_ref.at[pl.ds(moved_ref.shape[0] - TILE, TILE), pl.ds(0, HEAD_DIM)], line_ref, sem.at[0]
    )
    table.start()
    loads = [
        pltpu.make_async_copy(
            moved_ref.at[pl.ds(page * page_rows + half * page_len, page_len)],
            held_ref.at[page, half],
            sem.at[1 + 2 * page + half],
        )
        for page in range(pages)
        for half in range(2)
    ]
    for load in loads:
        load.start()
    row = lax.broadcasted_iota(jnp.int32, (TILE, HEAD_DIM), 0)
    held_ref[pages] = jnp.zeros(held_ref.shape[1:], held_ref.dtype)
    held_ref[pages, 0, page_len - TILE :, 0:HEAD_DIM] = jnp.full(
        (TILE, HEAD_DIM), MARK, held_ref.dtype
    )
    for slot in range(SPAN * CAPK):
        where_ref[slot] = pages
    for distance in range(SPAN):
        count_ref[distance] = 0
    table.wait()
    line = line_ref[...].astype(jnp.float32)
    lane = lax.broadcasted_iota(jnp.int32, (TILE, HEAD_DIM), 1)
    top = row == 0
    entries = [
        jnp.sum(jnp.where(top & (lane == i), line, 0.0)).astype(jnp.int32) for i in range(2 * pages)
    ]
    for page in range(pages):
        distance = entries[page]
        taken = count_ref[distance]
        where_ref[distance * CAPK + taken] = page
        count_ref[distance] = taken + 1
    for page in range(pages):
        loads[2 * page].wait()
        loads[2 * page + 1].wait()
        fill = entries[pages + page]
        tile = held_ref[page, 0, page_len - TILE :, 0:HEAD_DIM]
        marked = jnp.where(
            (row == TILE - 1) & (fill < page_len), MARK + fill.astype(jnp.float32), tile.astype(jnp.float32)
        )
        held_ref[page, 0, page_len - TILE :, 0:HEAD_DIM] = marked.astype(held_ref.dtype)
    stores = [
        pltpu.make_async_copy(
            held_ref.at[where_ref[distance * CAPK + j]],
            outs[distance].at[j],
            sem.at[1 + 2 * pages + distance * CAPK + j],
        )
        for distance in range(SPAN)
        for j in range(CAPK)
    ]
    for store in stores:
        store.start()
    for store in stores:
        store.wait()


def pack_pages(moved, pages, page_shape):
    shape = (CAPK,) + page_shape
    return pl.pallas_call(
        pack_kernel,
        in_specs=[ANY],
        out_specs=[ANY] * SPAN,
        out_shape=[jax.ShapeDtypeStruct(shape, moved.dtype)] * SPAN,
        scratch_shapes=[
            pltpu.VMEM((pages + 1,) + page_shape, moved.dtype),
            pltpu.VMEM((TILE, HEAD_DIM), moved.dtype),
            pltpu.SMEM((SPAN * CAPK,), jnp.int32),
            pltpu.SMEM((SPAN,), jnp.int32),
            pltpu.SemaphoreType.DMA((1 + 2 * pages + SPAN * CAPK,)),
        ],
        compiler_params=params(16),
        cost_estimate=pl.CostEstimate(flops=0, bytes_accessed=3 * 1024 * 1024, transcendentals=0),
        name="pack",
    )(moved)


def finish_kernel(away_ref, proj_ref, sum_ref, top_ref, total_ref, read_ref, lead_ref, w_ref, *rest):
    pages, states = rest[:SPAN], rest[SPAN:-4]
    out_ref, combined_ref, state_ref, sem = rest[-4:]
    away = away_ref[0]
    for i, state in enumerate(states):

        @pl.when(away == i)
        def _():
            pltpu.make_async_copy(state, state_ref, sem).start()

    page_len = pages[0].shape[2]
    row = lax.broadcasted_iota(jnp.int32, (page_len, HEAD_DIM), 0).astype(jnp.float32)
    hide = []
    for distance in range(SPAN):
        for j in range(CAPK):
            flag = pages[distance][j, 0, :, 0:HEAD_DIM].astype(jnp.float32)[
                page_len - 1 : page_len, 0:1
            ]
            fill = jnp.where(flag > MARK - 1.0, flag - MARK, float(page_len))
            hide.append(jnp.where(row < fill, 0.0, MASKED))
    hide = jnp.concatenate(hide, axis=0)[:, 0:1]
    for h in range(HEADS):
        cols = slice(h * HEAD_DIM, (h + 1) * HEAD_DIM)
        keys = jnp.concatenate(
            [pages[d][j, 0, :, cols] for d in range(SPAN) for j in range(CAPK)], axis=0
        )
        values = jnp.concatenate(
            [pages[d][j, 1, :, cols] for d in range(SPAN) for j in range(CAPK)], axis=0
        )
        s = nt(keys, proj_ref[:, cols]) + hide
        before = top_ref[h : h + 1, :]
        top = jnp.maximum(before, s.max(axis=0, keepdims=True))
        p = jnp.exp2(s * SCALE2 - top * SCALE2)
        shrink = jnp.exp2((before - top) * SCALE2)
        total = total_ref[h : h + 1, :] * shrink + p.sum(axis=0, keepdims=True)
        gathered = sum_ref[cols, :] * shrink + nn(jnp.transpose(values), p.astype(jnp.bfloat16))
        attended = jnp.transpose(gathered * (1.0 / total))
        if h == 0:
            pltpu.make_async_copy(states[0], state_ref, sem).wait()
        reads = read_ref[:, cols] + nt(lead_ref[:, cols], state_ref[h])
        combined_ref[:, cols] = (attended + reads).astype(jnp.bfloat16)
    out_ref[...] = nn(combined_ref[...], w_ref[...]).astype(jnp.bfloat16)


def finish(away, projected, own_sum, top, total, reads, leads, w_out, pages, states):
    width, length = own_sum.shape
    return pl.pallas_call(
        finish_kernel,
        grid=(1,),
        in_specs=[SMEM, pl.BlockSpec((length, width), lambda i: (0, 0))]
        + [VMEM] * (6 + SPAN)
        + [ANY] * len(states),
        out_specs=VMEM,
        out_shape=jax.ShapeDtypeStruct((length, w_out.shape[1]), jnp.bfloat16),
        scratch_shapes=[
            pltpu.VMEM((length, width), jnp.bfloat16),
            pltpu.VMEM(states[0].shape, states[0].dtype),
            pltpu.SemaphoreType.DMA,
        ],
        compiler_params=params(40),
        cost_estimate=pl.CostEstimate(
            flops=2 * length * width * (w_out.shape[1] + 768),
            bytes_accessed=16 * length * width,
            transcendentals=length * 384 * HEADS,
        ),
        name="finish",
    )(away, projected, own_sum, top, total, reads, leads, w_out, *pages, *states)


def shifted(block, axis, distance):
    size = lax.axis_size(axis)
    return lax.ppermute(block, axis, [((i - distance) % size, i) for i in range(size)])


def exchanged(block, axis, bit):
    return lax.ppermute(block, axis, [(i ^ bit, i) for i in range(lax.axis_size(axis))])


def migrate(code, payload, beside, arrays):
    groups = lax.axis_size("req")
    orders = list(itertools.permutations(range(groups)))

    def branch(order):
        route = [(order[g], g) for g in range(groups)]
        return lambda x, *xs: (lax.ppermute(x, "req", route),) + tuple(beside(*xs))

    return lax.switch(code, [branch(order) for order in orders], payload, *arrays)


def on_device(
    tokens,
    norm_gain,
    w_qkv,
    w_out,
    w_gates,
    gate_bias,
    persistent,
    cache,
    page_back,
    page_fill,
    mem_state,
    mig_source,
):
    pages = cache.shape[2]
    rows = cache.reshape(-1, cache.shape[-1])
    payload, code, away = prepare(mig_source, page_back, page_fill, rows)

    def beside(inputs, gain, w, wg, held):
        return tuple(project(inputs, gain, w, wg)) + (held.astype(jnp.bfloat16),)

    moved, projected, gates, state = migrate(
        code[0], payload, beside, (tokens[0, 0], norm_gain, w_qkv, w_gates, mem_state[0, 0])
    )
    near = exchanged(state, "req", 1)
    packed = pack_pages(moved, pages, cache.shape[3:])
    arrived = [packed[0]] + [shifted(packed[k], "seq", -k) for k in range(1, SPAN)]
    projected, near = lax.optimization_barrier((projected, near))
    own_sum, top, total = own_attention(projected, persistent)
    passed, _ = lax.optimization_barrier((jnp.where(away[1] == 1, near, state), top))
    far = exchanged(passed, "req", 2)
    reads, leads = memory_reads(projected, gates, gate_bias)
    result = finish(
        away, projected, own_sum, top, total, reads, leads, w_out, arrived, (state, near, far)
    )
    return result[None, None]


def solution(mesh):
    return jax.shard_map(
        on_device,
        mesh=mesh,
        in_specs=(
            P("req", "seq", None, None),
            P(),
            P(),
            P(),
            P(),
            P(),
            P(),
            P("req", "seq", None, None, None, None),
            P("req", "seq", None),
            P("req", "seq", None),
            P("req", "seq", None, None, None),
            P("seq", None),
        ),
        out_specs=P("req", "seq", None, None),
        check_vma=False,
    )
```

```python
import itertools

import jax
import jax.numpy as jnp
from jax import lax
from jax.experimental import pallas as pl
from jax.experimental.pallas import tpu as pltpu
from jax.sharding import PartitionSpec as P

HEADS = 8
HEAD_DIM = 128
BLK = 64
SPAN = 6
CAPK = 2
LOG2E = 1.4426950408889634
SCALE2 = HEAD_DIM ** (-0.5) * LOG2E
MASKED = -1e30
MARK = 128.0
TILE = 16
CHUNK = 128
VMEM = pl.BlockSpec(memory_space=pltpu.VMEM)
SMEM = pl.BlockSpec(memory_space=pltpu.SMEM)
ANY = pl.BlockSpec(memory_space=pl.ANY)


def nt(a, b):
    return lax.dot_general(a, b, (((1,), (1,)), ((), ())), preferred_element_type=jnp.float32)


def nn(a, b):
    return lax.dot_general(a, b, (((1,), (0,)), ((), ())), preferred_element_type=jnp.float32)


def params(mib):
    return pltpu.CompilerParams(vmem_limit_bytes=mib * 1024 * 1024)


def project_kernel(
    tokens_ref, gain_ref, w_ref, wg_ref, state_ref, out_ref, gates_ref, rounded_ref, normed_ref
):
    length = tokens_ref.shape[0]

    def chunk(i):
        return pl.ds(pl.multiple_of(i * CHUNK, CHUNK), CHUNK)

    @pl.when(pl.program_id(0) == 0)
    def _():
        @pl.loop(0, length // CHUNK)
        def _(i):
            rows = tokens_ref[chunk(i), :].astype(jnp.float32)
            mean = jnp.mean(rows * rows, axis=-1, keepdims=True)
            normed = (rows * lax.rsqrt(mean + 1e-05) * gain_ref[...]).astype(jnp.bfloat16)
            normed_ref[chunk(i), :] = normed
            gates_ref[chunk(i), :] = nn(normed, wg_ref[...])

        @pl.loop(0, HEADS)
        def _(h):
            rounded_ref[h] = state_ref[h].astype(jnp.bfloat16)

    @pl.loop(0, length // CHUNK)
    def _(i):
        out_ref[chunk(i), :] = nn(normed_ref[chunk(i), :], w_ref[...]).astype(jnp.bfloat16)


def project(tokens, gain, w_qkv, w_gates, state):
    length, width = tokens.shape
    columns = w_qkv.shape[1]
    tile = 512
    return pl.pallas_call(
        project_kernel,
        grid=(columns // tile,),
        in_specs=[
            pl.BlockSpec((length, width), lambda i: (0, 0)),
            pl.BlockSpec((1, width), lambda i: (0, 0)),
            pl.BlockSpec((width, tile), lambda i: (0, i)),
            pl.BlockSpec(w_gates.shape, lambda i: (0, 0)),
            pl.BlockSpec(state.shape, lambda i: (0, 0, 0)),
        ],
        out_specs=[
            pl.BlockSpec((length, tile), lambda i: (0, i)),
            pl.BlockSpec((length, w_gates.shape[1]), lambda i: (0, 0)),
            pl.BlockSpec(state.shape, lambda i: (0, 0, 0)),
        ],
        out_shape=[
            jax.ShapeDtypeStruct((length, columns), jnp.bfloat16),
            jax.ShapeDtypeStruct((length, w_gates.shape[1]), jnp.float32),
            jax.ShapeDtypeStruct(state.shape, jnp.bfloat16),
        ],
        scratch_shapes=[pltpu.VMEM((length, width), jnp.bfloat16)],
        compiler_params=params(24),
        cost_estimate=pl.CostEstimate(
            flops=2 * length * width * columns,
            bytes_accessed=2 * (width * columns + length * width + length * columns),
            transcendentals=0,
        ),
        name="project",
    )(tokens, gain.reshape(1, width), w_qkv, w_gates, state)


def own_kernel(proj_ref, lasting_ref, slots_ref, sum_ref, top_ref, total_ref):
    length = proj_ref.shape[0]
    width = HEADS * HEAD_DIM
    half = length // 2
    key = lax.broadcasted_iota(jnp.int32, (half, half), 0)
    token = lax.broadcasted_iota(jnp.int32, (half, half), 1)
    causal = key <= token
    hide = hidden(slots_ref)
    for h in range(HEADS):
        cols = slice(h * HEAD_DIM, (h + 1) * HEAD_DIM)
        keys = proj_ref[:, width + h * HEAD_DIM : width + (h + 1) * HEAD_DIM]
        page_keys = jnp.concatenate(slot_rows(slots_ref, 0, cols), axis=0)
        values = jnp.concatenate(
            slot_rows(slots_ref, 1, cols)
            + [
                lasting_ref[1, :, cols],
                proj_ref[:, 2 * width + h * HEAD_DIM : 2 * width + (h + 1) * HEAD_DIM],
            ],
            axis=0,
        )
        turned = jnp.transpose(values)
        for part in range(2):
            rows = slice(part * half, (part + 1) * half)
            q = proj_ref[rows, cols]
            scores = [nt(page_keys, q) + hide, nt(lasting_ref[0, :, cols], q)]
            scores += [nt(keys[i * half : (i + 1) * half], q) for i in range(part)]
            scores.append(jnp.where(causal, nt(keys[rows], q), MASKED))
            top = scores[1].max(axis=0, keepdims=True)
            for s in scores[:1] + scores[2:]:
                top = jnp.maximum(top, s.max(axis=0, keepdims=True))
            shift = top * SCALE2
            weights = [jnp.exp2(s * SCALE2 - shift) for s in scores]
            total = weights[0].sum(axis=0, keepdims=True)
            for w in weights[1:]:
                total = total + w.sum(axis=0, keepdims=True)
            rounded = jnp.concatenate([w.astype(jnp.bfloat16) for w in weights], axis=0)
            sum_ref[cols, rows] = nn(turned[:, : rounded.shape[0]], rounded)
            top_ref[h : h + 1, rows] = top
            total_ref[h : h + 1, rows] = total


def own_attention(projected, persistent, slots):
    length = projected.shape[0]
    width = HEADS * HEAD_DIM
    return pl.pallas_call(
        own_kernel,
        in_specs=[VMEM, VMEM, VMEM],
        out_specs=[VMEM, VMEM, VMEM],
        out_shape=[
            jax.ShapeDtypeStruct((width, length), jnp.float32),
            jax.ShapeDtypeStruct((HEADS, length), jnp.float32),
            jax.ShapeDtypeStruct((HEADS, length), jnp.float32),
        ],
        compiler_params=params(32),
        cost_estimate=pl.CostEstimate(
            flops=3 * length * length * width,
            bytes_accessed=10 * length * width,
            transcendentals=length * length * HEADS,
        ),
        name="own",
    )(projected, persistent, slots)


def memory_kernel(proj_ref, gates_ref, bias_ref, out_ref, lead_ref, mem_ref):
    length = proj_ref.shape[0]
    width = HEADS * HEAD_DIM
    blocks = length // BLK
    means = jnp.concatenate(
        [jnp.mean(gates_ref[b * BLK : (b + 1) * BLK, :], axis=0, keepdims=True) for b in range(blocks)],
        axis=0,
    )
    decay = 1.0 / (1.0 + jnp.exp(means[:, :HEADS] + bias_ref[0:1, :] - 2.5))
    rate = 0.5 / (1.0 + jnp.exp(-(means[:, HEADS : 2 * HEADS] + bias_ref[1:2, :])))
    mix = 1.0 / (1.0 + jnp.exp(-(gates_ref[:, 2 * HEADS :] + bias_ref[2:3, :])))
    one = lax.broadcasted_iota(jnp.int32, (HEAD_DIM, HEAD_DIM), 0) == lax.broadcasted_iota(
        jnp.int32, (HEAD_DIM, HEAD_DIM), 1
    )
    for b in range(blocks):
        rows = slice(b * BLK, (b + 1) * BLK)
        for h in range(HEADS):
            cols = slice(h * HEAD_DIM, (h + 1) * HEAD_DIM)
            q = proj_ref[rows, cols]
            k = proj_ref[rows, slice(width + h * HEAD_DIM, width + (h + 1) * HEAD_DIM)]
            v = proj_ref[rows, slice(2 * width + h * HEAD_DIM, 2 * width + (h + 1) * HEAD_DIM)]
            qf, kf = q.astype(jnp.float32), k.astype(jnp.float32)
            unit_q = lax.rsqrt(jnp.sum(qf * qf, axis=1, keepdims=True) + 1e-06) * mix[rows, h : h + 1]
            unit_k = lax.rsqrt(jnp.sum(kf * kf, axis=1, keepdims=True) + 1e-06)
            fade = decay[b : b + 1, h : h + 1]
            if b == 0:
                out_ref[rows, cols] = jnp.zeros((BLK, HEAD_DIM), jnp.float32)
                lead_ref[rows, cols] = (qf * unit_q).astype(jnp.bfloat16)
                held = kf * unit_k
                kept = jnp.concatenate(
                    [jnp.zeros((HEAD_DIM, HEAD_DIM), jnp.float32), jnp.where(one, fade, 0.0)], axis=1
                )
                error = jnp.concatenate([-v.astype(jnp.float32), held], axis=1)
            else:
                mem = mem_ref[h]
                both = nn(jnp.concatenate([q, k], axis=0), mem.astype(jnp.bfloat16))
                out_ref[rows, cols] = both[:BLK, :HEAD_DIM] * unit_q
                lead_ref[rows, cols] = (both[:BLK, HEAD_DIM:] * unit_q).astype(jnp.bfloat16)
                if b == blocks - 1:
                    continue
                kept = mem * fade
                error = jnp.concatenate(
                    [
                        both[BLK:, :HEAD_DIM] * unit_k - v.astype(jnp.float32),
                        both[BLK:, HEAD_DIM:] * unit_k,
                    ],
                    axis=1,
                )
            step = error * (unit_k * -rate[b : b + 1, h : h + 1])
            mem_ref[h] = kept + nn(jnp.transpose(kf).astype(jnp.bfloat16), step.astype(jnp.bfloat16))


def memory_reads(projected, gates, gate_bias):
    length = projected.shape[0]
    width = HEADS * HEAD_DIM
    return pl.pallas_call(
        memory_kernel,
        in_specs=[VMEM] * 3,
        out_specs=[VMEM] * 2,
        out_shape=[
            jax.ShapeDtypeStruct((length, width), jnp.float32),
            jax.ShapeDtypeStruct((length, width), jnp.bfloat16),
        ],
        scratch_shapes=[pltpu.VMEM((HEADS, HEAD_DIM, 2 * HEAD_DIM), jnp.float32)],
        compiler_params=params(32),
        cost_estimate=pl.CostEstimate(
            flops=12 * length * HEAD_DIM * width,
            bytes_accessed=12 * length * width,
            transcendentals=0,
        ),
        name="memory",
    )(projected, gates, gate_bias)


def prepare_kernel(
    sources_ref, back_ref, fill_ref, cache_ref, out_ref, code_ref, away_ref,
    order_ref, place_ref, used_ref, where_ref, count_ref, held_ref, sem,
):
    cached = cache_ref.shape[0]
    pages = back_ref.shape[2]
    page_rows = cached // pages
    page_len = page_rows // 2
    groups = sources_ref.shape[1]
    whole = pltpu.make_async_copy(cache_ref, held_ref.at[pl.ds(0, cached)], sem.at[3])
    whole.start()
    loads = [
        pltpu.make_async_copy(sources_ref, order_ref, sem.at[0]),
        pltpu.make_async_copy(back_ref.at[0], place_ref, sem.at[1]),
        pltpu.make_async_copy(fill_ref.at[0], used_ref, sem.at[2]),
    ]
    for load in loads:
        load.start()
    for slot in range(SPAN * CAPK):
        where_ref[slot] = pages
    for distance in range(SPAN):
        count_ref[distance] = 0
    for load in loads:
        load.wait()
    code = jnp.int32(0)
    for g in range(groups - 1):
        smaller = jnp.int32(0)
        for later in range(g + 1, groups):
            smaller = smaller + (order_ref[0, later] < order_ref[0, g]).astype(jnp.int32)
        code = code * (groups - g) + smaller
    code_ref[0] = code
    here = lax.axis_index("req")
    source, near = order_ref[0, here], here ^ 1
    away_ref[0] = jnp.where(source == here, 0, jnp.where(source == near, 1, 2))
    away_ref[1] = (order_ref[0, here ^ 2] == near).astype(jnp.int32)
    for page in range(pages):
        distance = place_ref[0, page]
        taken = count_ref[distance]
        where_ref[distance * CAPK + taken] = page
        count_ref[distance] = taken + 1
    lane = lax.broadcasted_iota(jnp.int32, (TILE, HEAD_DIM), 1)
    row = lax.broadcasted_iota(jnp.int32, (TILE, HEAD_DIM), 0)
    line = jnp.zeros((TILE, HEAD_DIM), jnp.float32)
    for distance in range(SPAN):
        entry = where_ref[distance * CAPK] * 16 + where_ref[distance * CAPK + 1]
        line = jnp.where(lane == distance, entry.astype(jnp.float32), line)
    held_ref[cached:, :] = jnp.zeros((TILE, held_ref.shape[1]), jnp.bfloat16)
    held_ref[cached:, 0:HEAD_DIM] = line.astype(jnp.bfloat16)
    whole.wait()
    for page in range(pages):
        fill = used_ref[0, page]
        last = slice(page * page_rows + page_len - TILE, page * page_rows + page_len)
        marked = jnp.where(
            (row == TILE - 1) & (fill < page_len),
            MARK + fill.astype(jnp.float32),
            held_ref[last, 0:HEAD_DIM].astype(jnp.float32),
        )
        held_ref[last, 0:HEAD_DIM] = marked.astype(jnp.bfloat16)
    store = pltpu.make_async_copy(held_ref, out_ref, sem.at[4])
    store.start()
    store.wait()


def prepare(sources, back, fill, cache):
    cached, width = cache.shape
    pages = back.shape[2]
    return pl.pallas_call(
        prepare_kernel,
        in_specs=[ANY] * 4,
        out_specs=[ANY, SMEM, SMEM],
        out_shape=[
            jax.ShapeDtypeStruct((cached + TILE, width), cache.dtype),
            jax.ShapeDtypeStruct((1,), jnp.int32),
            jax.ShapeDtypeStruct((2,), jnp.int32),
        ],
        scratch_shapes=[
            pltpu.SMEM(sources.shape, jnp.int32),
            pltpu.SMEM((1, pages), jnp.int32),
            pltpu.SMEM((1, pages), jnp.int32),
            pltpu.SMEM((SPAN * CAPK,), jnp.int32),
            pltpu.SMEM((SPAN,), jnp.int32),
            pltpu.VMEM((cached + TILE, width), cache.dtype),
            pltpu.SemaphoreType.DMA((5,)),
        ],
        compiler_params=params(56),
        cost_estimate=pl.CostEstimate(flops=0, bytes_accessed=2 * 1024 * 1024, transcendentals=0),
        name="prepare",
    )(sources, back, fill, cache)


def pack_kernel(moved_ref, *rest):
    outs = rest[:SPAN]
    held_ref, line_ref, sem = rest[SPAN:]
    page_len = outs[0].shape[2]
    pages = held_ref.shape[0] - 1
    cached = moved_ref.shape[0] - TILE
    table = pltpu.make_async_copy(
        moved_ref.at[pl.ds(cached, TILE), pl.ds(0, HEAD_DIM)], line_ref, sem.at[0]
    )
    table.start()
    loads = [
        pltpu.make_async_copy(
            moved_ref.at[pl.ds(half * page_len, page_len)],
            held_ref.at[half // 2, half % 2],
            sem.at[1 + half],
        )
        for half in range(2 * pages)
    ]
    for load in loads:
        load.start()
    held_ref[pages] = jnp.zeros(held_ref.shape[1:], held_ref.dtype)
    held_ref[pages, 0, page_len - TILE :, 0:HEAD_DIM] = jnp.full(
        (TILE, HEAD_DIM), MARK, held_ref.dtype
    )
    table.wait()
    line = line_ref[0:8, :].astype(jnp.float32)
    lane = lax.broadcasted_iota(jnp.int32, line.shape, 1)
    entries = [
        jnp.max(jnp.where(lane == distance, line, 0.0)).astype(jnp.int32) for distance in range(SPAN)
    ]
    for load in loads:
        load.wait()
    stores = []
    for distance in range(SPAN):
        for j, page in enumerate((entries[distance] // 16, entries[distance] % 16)):
            stores.append(
                pltpu.make_async_copy(
                    held_ref.at[page],
                    outs[distance].at[j],
                    sem.at[1 + 2 * pages + distance * CAPK + j],
                )
            )
            stores[-1].start()
    for store in stores:
        store.wait()


def pack_pages(moved, pages, page_shape):
    shape = (CAPK,) + page_shape
    return pl.pallas_call(
        pack_kernel,
        in_specs=[ANY],
        out_specs=[ANY] * SPAN,
        out_shape=[jax.ShapeDtypeStruct(shape, moved.dtype)] * SPAN,
        scratch_shapes=[
            pltpu.VMEM((pages + 1,) + page_shape, moved.dtype),
            pltpu.VMEM((TILE, HEAD_DIM), moved.dtype),
            pltpu.SemaphoreType.DMA((1 + 2 * pages + SPAN * CAPK,)),
        ],
        compiler_params=params(16),
        cost_estimate=pl.CostEstimate(flops=0, bytes_accessed=3 * 1024 * 1024, transcendentals=0),
        name="pack",
    )(moved)


def hidden(slots):
    page_len = slots.shape[2]
    row = lax.broadcasted_iota(jnp.int32, (page_len, HEAD_DIM), 0).astype(jnp.float32)
    parts = []
    for j in range(CAPK):
        tile = slots[j, 0, page_len - TILE :, 0:HEAD_DIM].astype(jnp.float32)
        flag = tile[TILE - 1 : TILE, 0:1]
        fill = jnp.where(flag > MARK - 1.0, flag - MARK, float(page_len))
        parts.append(jnp.where(row < fill, 0.0, MASKED))
    return jnp.concatenate(parts, axis=0)[:, 0:1]


def slot_rows(slots, which, cols):
    return [slots[j, which, :, cols] for j in range(CAPK)]


def finish_kernel(away_ref, proj_ref, sum_ref, top_ref, total_ref, read_ref, lead_ref, w_ref, *rest):
    pages, states = rest[: SPAN - 1], rest[SPAN - 1 : -4]
    out_ref, combined_ref, state_ref, sem = rest[-4:]
    away = away_ref[0]
    for i, state in enumerate(states):

        @pl.when(away == i)
        def _():
            pltpu.make_async_copy(state, state_ref, sem).start()

    hide = jnp.concatenate([hidden(slots) for slots in pages], axis=0)
    for h in range(HEADS):
        cols = slice(h * HEAD_DIM, (h + 1) * HEAD_DIM)
        keys = jnp.concatenate(sum((slot_rows(slots, 0, cols) for slots in pages), []), axis=0)
        values = jnp.concatenate(sum((slot_rows(slots, 1, cols) for slots in pages), []), axis=0)
        s = nt(keys, proj_ref[:, cols]) + hide
        before = top_ref[h : h + 1, :]
        top = jnp.maximum(before, s.max(axis=0, keepdims=True))
        p = jnp.exp2(s * SCALE2 - top * SCALE2)
        shrink = jnp.exp2((before - top) * SCALE2)
        total = total_ref[h : h + 1, :] * shrink + p.sum(axis=0, keepdims=True)
        gathered = sum_ref[cols, :] * shrink + nn(jnp.transpose(values), p.astype(jnp.bfloat16))
        attended = jnp.transpose(gathered * (1.0 / total))
        if h == 0:
            pltpu.make_async_copy(states[0], state_ref, sem).wait()
        reads = read_ref[:, cols] + nt(lead_ref[:, cols], state_ref[h])
        combined_ref[:, cols] = (attended + reads).astype(jnp.bfloat16)
    out_ref[...] = nn(combined_ref[...], w_ref[...]).astype(jnp.bfloat16)


def finish(away, projected, own_sum, top, total, reads, leads, w_out, pages, states):
    width, length = own_sum.shape
    return pl.pallas_call(
        finish_kernel,
        grid=(1,),
        in_specs=[SMEM, pl.BlockSpec((length, width), lambda i: (0, 0))]
        + [VMEM] * (6 + len(pages))
        + [ANY] * len(states),
        out_specs=VMEM,
        out_shape=jax.ShapeDtypeStruct((length, w_out.shape[1]), jnp.bfloat16),
        scratch_shapes=[
            pltpu.VMEM((length, width), jnp.bfloat16),
            pltpu.VMEM(states[0].shape, states[0].dtype),
            pltpu.SemaphoreType.DMA,
        ],
        compiler_params=params(40),
        cost_estimate=pl.CostEstimate(
            flops=2 * length * width * (w_out.shape[1] + 768),
            bytes_accessed=16 * length * width,
            transcendentals=length * 384 * HEADS,
        ),
        name="finish",
    )(away, projected, own_sum, top, total, reads, leads, w_out, *pages, *states)


def shifted(block, axis, distance):
    size = lax.axis_size(axis)
    return lax.ppermute(block, axis, [((i - distance) % size, i) for i in range(size)])


def exchanged(block, axis, bit):
    return lax.ppermute(block, axis, [(i ^ bit, i) for i in range(lax.axis_size(axis))])


def migrate(code, payload, beside, arrays):
    groups = lax.axis_size("req")
    orders = list(itertools.permutations(range(groups)))

    def branch(order):
        route = [(order[g], g) for g in range(groups)]
        return lambda x, *xs: (lax.ppermute(x, "req", route),) + tuple(beside(*xs))

    return lax.switch(code, [branch(order) for order in orders], payload, *arrays)


def on_device(
    tokens,
    norm_gain,
    w_qkv,
    w_out,
    w_gates,
    gate_bias,
    persistent,
    cache,
    page_back,
    page_fill,
    mem_state,
    mig_source,
):
    pages = cache.shape[2]
    rows = cache.reshape(-1, cache.shape[-1])
    payload, code, away = prepare(mig_source, page_back, page_fill, rows)
    moved, projected, gates, state = migrate(
        code[0], payload, project, (tokens[0, 0], norm_gain, w_qkv, w_gates, mem_state[0, 0])
    )
    near = exchanged(state, "req", 1)
    packed = pack_pages(moved, pages, cache.shape[3:])
    arrived = [shifted(packed[k], "seq", -k) for k in range(1, SPAN)]
    projected, near = lax.optimization_barrier((projected, near))
    own_sum, top, total = own_attention(projected, persistent, packed[0])
    passed, _ = lax.optimization_barrier((jnp.where(away[1] == 1, near, state), top))
    far = exchanged(passed, "req", 2)
    reads, leads = memory_reads(projected, gates, gate_bias)
    result = finish(
        away, projected, own_sum, top, total, reads, leads, w_out, arrived, (state, near, far)
    )
    return result[None, None]


def solution(mesh):
    return jax.shard_map(
        on_device,
        mesh=mesh,
        in_specs=(
            P("req", "seq", None, None),
            P(),
            P(),
            P(),
            P(),
            P(),
            P(),
            P("req", "seq", None, None, None, None),
            P("req", "seq", None),
            P("req", "seq", None),
            P("req", "seq", None, None, None),
            P("seq", None),
        ),
        out_specs=P("req", "seq", None, None),
        check_vma=False,
    )
```

```python
import itertools

import jax
import jax.numpy as jnp
from jax import lax
from jax.experimental import pallas as pl
from jax.experimental.pallas import tpu as pltpu
from jax.sharding import PartitionSpec as P

HEADS = 8
HEAD_DIM = 128
BLK = 64
SPAN = 6
CAPK = 2
LOG2E = 1.4426950408889634
SCALE2 = HEAD_DIM ** (-0.5) * LOG2E
MASKED = -1e30
MARK = 128.0
TILE = 16
CHUNK = 128
VMEM = pl.BlockSpec(memory_space=pltpu.VMEM)
SMEM = pl.BlockSpec(memory_space=pltpu.SMEM)
ANY = pl.BlockSpec(memory_space=pl.ANY)


def nt(a, b):
    return lax.dot_general(a, b, (((1,), (1,)), ((), ())), preferred_element_type=jnp.float32)


def nn(a, b):
    return lax.dot_general(a, b, (((1,), (0,)), ((), ())), preferred_element_type=jnp.float32)


def params(mib):
    return pltpu.CompilerParams(vmem_limit_bytes=mib * 1024 * 1024)


def project_kernel(
    tokens_ref, gain_ref, w_ref, wg_ref, state_ref, out_ref, gates_ref, rounded_ref, normed_ref
):
    length = tokens_ref.shape[0]

    def chunk(i):
        return pl.ds(pl.multiple_of(i * CHUNK, CHUNK), CHUNK)

    @pl.when(pl.program_id(0) == 0)
    def _():
        @pl.loop(0, length // CHUNK)
        def _(i):
            rows = tokens_ref[chunk(i), :].astype(jnp.float32)
            mean = jnp.mean(rows * rows, axis=-1, keepdims=True)
            normed = (rows * lax.rsqrt(mean + 1e-05) * gain_ref[...]).astype(jnp.bfloat16)
            normed_ref[chunk(i), :] = normed
            gates_ref[chunk(i), :] = nt(normed, wg_ref[...])

        @pl.loop(0, HEADS)
        def _(h):
            rounded_ref[h] = state_ref[h].astype(jnp.bfloat16)

    @pl.loop(0, length // CHUNK)
    def _(i):
        out_ref[chunk(i), :] = nn(normed_ref[chunk(i), :], w_ref[...]).astype(jnp.bfloat16)


def project(tokens, gain, w_qkv, gates_turned, state):
    length, width = tokens.shape
    columns = w_qkv.shape[1]
    tile = 512
    return pl.pallas_call(
        project_kernel,
        grid=(columns // tile,),
        in_specs=[
            pl.BlockSpec((length, width), lambda i: (0, 0)),
            pl.BlockSpec((1, width), lambda i: (0, 0)),
            pl.BlockSpec((width, tile), lambda i: (0, i)),
            pl.BlockSpec(gates_turned.shape, lambda i: (0, 0)),
            pl.BlockSpec(state.shape, lambda i: (0, 0, 0)),
        ],
        out_specs=[
            pl.BlockSpec((length, tile), lambda i: (0, i)),
            pl.BlockSpec((length, gates_turned.shape[0]), lambda i: (0, 0)),
            pl.BlockSpec(state.shape, lambda i: (0, 0, 0)),
        ],
        out_shape=[
            jax.ShapeDtypeStruct((length, columns), jnp.bfloat16),
            jax.ShapeDtypeStruct((length, gates_turned.shape[0]), jnp.float32),
            jax.ShapeDtypeStruct(state.shape, jnp.bfloat16),
        ],
        scratch_shapes=[pltpu.VMEM((length, width), jnp.bfloat16)],
        compiler_params=params(24),
        cost_estimate=pl.CostEstimate(
            flops=2 * length * width * columns,
            bytes_accessed=2 * (width * columns + length * width + length * columns),
            transcendentals=0,
        ),
        name="project",
    )(tokens, gain.reshape(1, width), w_qkv, gates_turned, state)


def own_kernel(proj_ref, lasting_ref, slots_ref, sum_ref, top_ref, total_ref):
    length = proj_ref.shape[0]
    width = HEADS * HEAD_DIM
    half = length // 2
    key = lax.broadcasted_iota(jnp.int32, (half, half), 0)
    token = lax.broadcasted_iota(jnp.int32, (half, half), 1)
    causal = key <= token
    hide = hidden(slots_ref)
    for h in range(HEADS):
        cols = slice(h * HEAD_DIM, (h + 1) * HEAD_DIM)
        keys = proj_ref[:, width + h * HEAD_DIM : width + (h + 1) * HEAD_DIM]
        page_keys = jnp.concatenate(slot_rows(slots_ref, 0, cols), axis=0)
        values = jnp.concatenate(
            slot_rows(slots_ref, 1, cols)
            + [
                lasting_ref[1, :, cols],
                proj_ref[:, 2 * width + h * HEAD_DIM : 2 * width + (h + 1) * HEAD_DIM],
            ],
            axis=0,
        )
        turned = jnp.transpose(values)
        for part in range(2):
            rows = slice(part * half, (part + 1) * half)
            q = proj_ref[rows, cols]
            scores = [nt(page_keys, q) + hide, nt(lasting_ref[0, :, cols], q)]
            scores += [nt(keys[i * half : (i + 1) * half], q) for i in range(part)]
            scores.append(jnp.where(causal, nt(keys[rows], q), MASKED))
            top = scores[1].max(axis=0, keepdims=True)
            for s in scores[:1] + scores[2:]:
                top = jnp.maximum(top, s.max(axis=0, keepdims=True))
            shift = top * SCALE2
            weights = [jnp.exp2(s * SCALE2 - shift) for s in scores]
            total = weights[0].sum(axis=0, keepdims=True)
            for w in weights[1:]:
                total = total + w.sum(axis=0, keepdims=True)
            rounded = jnp.concatenate([w.astype(jnp.bfloat16) for w in weights], axis=0)
            sum_ref[cols, rows] = nn(turned[:, : rounded.shape[0]], rounded)
            top_ref[h : h + 1, rows] = top
            total_ref[h : h + 1, rows] = total


def own_attention(projected, persistent, slots):
    length = projected.shape[0]
    width = HEADS * HEAD_DIM
    return pl.pallas_call(
        own_kernel,
        in_specs=[VMEM, VMEM, VMEM],
        out_specs=[VMEM, VMEM, VMEM],
        out_shape=[
            jax.ShapeDtypeStruct((width, length), jnp.float32),
            jax.ShapeDtypeStruct((HEADS, length), jnp.float32),
            jax.ShapeDtypeStruct((HEADS, length), jnp.float32),
        ],
        compiler_params=params(32),
        cost_estimate=pl.CostEstimate(
            flops=3 * length * length * width,
            bytes_accessed=10 * length * width,
            transcendentals=length * length * HEADS,
        ),
        name="own",
    )(projected, persistent, slots)


def memory_kernel(proj_ref, gates_ref, bias_ref, out_ref, lead_ref, mem_ref):
    length = proj_ref.shape[0]
    width = HEADS * HEAD_DIM
    blocks = length // BLK
    means = jnp.concatenate(
        [jnp.mean(gates_ref[b * BLK : (b + 1) * BLK, :], axis=0, keepdims=True) for b in range(blocks)],
        axis=0,
    )
    decay = 1.0 / (1.0 + jnp.exp(means[:, :HEADS] + bias_ref[0:1, :] - 2.5))
    rate = 0.5 / (1.0 + jnp.exp(-(means[:, HEADS : 2 * HEADS] + bias_ref[1:2, :])))
    mix = 1.0 / (1.0 + jnp.exp(-(gates_ref[:, 2 * HEADS :] + bias_ref[2:3, :])))
    one = lax.broadcasted_iota(jnp.int32, (HEAD_DIM, HEAD_DIM), 0) == lax.broadcasted_iota(
        jnp.int32, (HEAD_DIM, HEAD_DIM), 1
    )
    for b in range(blocks):
        rows = slice(b * BLK, (b + 1) * BLK)
        for h in range(HEADS):
            cols = slice(h * HEAD_DIM, (h + 1) * HEAD_DIM)
            q = proj_ref[rows, cols]
            k = proj_ref[rows, slice(width + h * HEAD_DIM, width + (h + 1) * HEAD_DIM)]
            v = proj_ref[rows, slice(2 * width + h * HEAD_DIM, 2 * width + (h + 1) * HEAD_DIM)]
            qf, kf = q.astype(jnp.float32), k.astype(jnp.float32)
            unit_q = lax.rsqrt(jnp.sum(qf * qf, axis=1, keepdims=True) + 1e-06) * mix[rows, h : h + 1]
            unit_k = lax.rsqrt(jnp.sum(kf * kf, axis=1, keepdims=True) + 1e-06)
            fade = decay[b : b + 1, h : h + 1]
            if b == 0:
                out_ref[rows, cols] = jnp.zeros((BLK, HEAD_DIM), jnp.float32)
                lead_ref[rows, cols] = (qf * unit_q).astype(jnp.bfloat16)
                held = kf * unit_k
                kept = jnp.concatenate(
                    [jnp.zeros((HEAD_DIM, HEAD_DIM), jnp.float32), jnp.where(one, fade, 0.0)], axis=1
                )
                error = jnp.concatenate([-v.astype(jnp.float32), held], axis=1)
            else:
                mem = mem_ref[h]
                both = nn(jnp.concatenate([q, k], axis=0), mem.astype(jnp.bfloat16))
                out_ref[rows, cols] = both[:BLK, :HEAD_DIM] * unit_q
                lead_ref[rows, cols] = (both[:BLK, HEAD_DIM:] * unit_q).astype(jnp.bfloat16)
                if b == blocks - 1:
                    continue
                kept = mem * fade
                error = jnp.concatenate(
                    [
                        both[BLK:, :HEAD_DIM] * unit_k - v.astype(jnp.float32),
                        both[BLK:, HEAD_DIM:] * unit_k,
                    ],
                    axis=1,
                )
            step = error * (unit_k * -rate[b : b + 1, h : h + 1])
            mem_ref[h] = kept + nn(jnp.transpose(kf).astype(jnp.bfloat16), step.astype(jnp.bfloat16))


def memory_reads(projected, gates, gate_bias):
    length = projected.shape[0]
    width = HEADS * HEAD_DIM
    return pl.pallas_call(
        memory_kernel,
        in_specs=[VMEM] * 3,
        out_specs=[VMEM] * 2,
        out_shape=[
            jax.ShapeDtypeStruct((length, width), jnp.float32),
            jax.ShapeDtypeStruct((length, width), jnp.bfloat16),
        ],
        scratch_shapes=[pltpu.VMEM((HEADS, HEAD_DIM, 2 * HEAD_DIM), jnp.float32)],
        compiler_params=params(32),
        cost_estimate=pl.CostEstimate(
            flops=12 * length * HEAD_DIM * width,
            bytes_accessed=12 * length * width,
            transcendentals=0,
        ),
        name="memory",
    )(projected, gates, gate_bias)


def prepare_kernel(
    sources_ref, back_ref, fill_ref, cache_ref, out_ref, code_ref, away_ref,
    order_ref, place_ref, used_ref, where_ref, count_ref, held_ref, sem,
):
    cached = cache_ref.shape[0]
    pages = back_ref.shape[2]
    page_rows = cached // pages
    page_len = page_rows // 2
    groups = sources_ref.shape[1]
    whole = pltpu.make_async_copy(cache_ref, held_ref.at[pl.ds(0, cached)], sem.at[3])
    whole.start()
    loads = [
        pltpu.make_async_copy(sources_ref, order_ref, sem.at[0]),
        pltpu.make_async_copy(back_ref.at[0], place_ref, sem.at[1]),
        pltpu.make_async_copy(fill_ref.at[0], used_ref, sem.at[2]),
    ]
    for load in loads:
        load.start()
    for slot in range(SPAN * CAPK):
        where_ref[slot] = pages
    for distance in range(SPAN):
        count_ref[distance] = 0
    for load in loads:
        load.wait()
    code = jnp.int32(0)
    for g in range(groups - 1):
        smaller = jnp.int32(0)
        for later in range(g + 1, groups):
            smaller = smaller + (order_ref[0, later] < order_ref[0, g]).astype(jnp.int32)
        code = code * (groups - g) + smaller
    code_ref[0] = code
    here = lax.axis_index("req")
    source, near = order_ref[0, here], here ^ 1
    away_ref[0] = jnp.where(source == here, 0, jnp.where(source == near, 1, 2))
    away_ref[1] = (order_ref[0, here ^ 2] == near).astype(jnp.int32)
    for page in range(pages):
        distance = place_ref[0, page]
        taken = count_ref[distance]
        where_ref[distance * CAPK + taken] = page
        count_ref[distance] = taken + 1
    lane = lax.broadcasted_iota(jnp.int32, (TILE, HEAD_DIM), 1)
    row = lax.broadcasted_iota(jnp.int32, (TILE, HEAD_DIM), 0)
    line = jnp.zeros((TILE, HEAD_DIM), jnp.float32)
    for distance in range(SPAN):
        entry = where_ref[distance * CAPK] * 16 + where_ref[distance * CAPK + 1]
        line = jnp.where(lane == distance, entry.astype(jnp.float32), line)
    held_ref[cached:, :] = jnp.zeros((TILE, held_ref.shape[1]), jnp.bfloat16)
    held_ref[cached:, 0:HEAD_DIM] = line.astype(jnp.bfloat16)
    whole.wait()
    for page in range(pages):
        fill = used_ref[0, page]
        last = slice(page * page_rows + page_len - TILE, page * page_rows + page_len)
        marked = jnp.where(
            (row == TILE - 1) & (fill < page_len),
            MARK + fill.astype(jnp.float32),
            held_ref[last, 0:HEAD_DIM].astype(jnp.float32),
        )
        held_ref[last, 0:HEAD_DIM] = marked.astype(jnp.bfloat16)
    store = pltpu.make_async_copy(held_ref, out_ref, sem.at[4])
    store.start()
    store.wait()


def prepare(sources, back, fill, cache):
    cached, width = cache.shape
    pages = back.shape[2]
    return pl.pallas_call(
        prepare_kernel,
        in_specs=[ANY] * 4,
        out_specs=[ANY, SMEM, SMEM],
        out_shape=[
            jax.ShapeDtypeStruct((cached + TILE, width), cache.dtype),
            jax.ShapeDtypeStruct((1,), jnp.int32),
            jax.ShapeDtypeStruct((2,), jnp.int32),
        ],
        scratch_shapes=[
            pltpu.SMEM(sources.shape, jnp.int32),
            pltpu.SMEM((1, pages), jnp.int32),
            pltpu.SMEM((1, pages), jnp.int32),
            pltpu.SMEM((SPAN * CAPK,), jnp.int32),
            pltpu.SMEM((SPAN,), jnp.int32),
            pltpu.VMEM((cached + TILE, width), cache.dtype),
            pltpu.SemaphoreType.DMA((5,)),
        ],
        compiler_params=params(56),
        cost_estimate=pl.CostEstimate(flops=0, bytes_accessed=2 * 1024 * 1024, transcendentals=0),
        name="prepare",
    )(sources, back, fill, cache)


def pack_kernel(moved_ref, *rest):
    outs = rest[:SPAN]
    line_ref, sem = rest[SPAN:]
    page_len = outs[0].shape[2]
    page_rows = 2 * page_len
    cached = moved_ref.shape[0] - TILE
    pages = cached // page_rows
    table = pltpu.make_async_copy(
        moved_ref.at[pl.ds(cached, TILE), pl.ds(0, HEAD_DIM)], line_ref, sem.at[SPAN]
    )
    table.start()
    table.wait()
    line = line_ref[0:8, :].astype(jnp.float32)
    lane = lax.broadcasted_iota(jnp.int32, line.shape, 1)
    entries = [
        jnp.max(jnp.where(lane == distance, line, 0.0)).astype(jnp.int32) for distance in range(SPAN)
    ]
    for distance in range(SPAN):
        for j, page in enumerate((entries[distance] >> 4, entries[distance] & 15)):

            @pl.when(page < pages)
            def _():
                for half in range(2):
                    start = pl.multiple_of(page * page_rows + half * page_len, page_len)
                    pltpu.make_async_copy(
                        moved_ref.at[pl.ds(start, page_len)], outs[distance].at[j, half], sem.at[distance]
                    ).start()

            @pl.when(page >= pages)
            def _():
                outs[distance][j] = jnp.zeros(outs[distance].shape[1:], moved_ref.dtype)
                outs[distance][j, 0, page_len - TILE :, 0:HEAD_DIM] = jnp.full(
                    (TILE, HEAD_DIM), MARK, moved_ref.dtype
                )

    for distance in range(SPAN):
        for j, page in enumerate((entries[distance] >> 4, entries[distance] & 15)):

            @pl.when(page < pages)
            def _():
                for half in range(2):
                    pltpu.make_async_copy(
                        moved_ref.at[pl.ds(0, page_len)], outs[distance].at[j, half], sem.at[distance]
                    ).wait()


def pack_pages(moved, pages, page_shape):
    shape = (CAPK,) + page_shape
    return pl.pallas_call(
        pack_kernel,
        in_specs=[ANY],
        out_specs=[VMEM] * SPAN,
        out_shape=[jax.ShapeDtypeStruct(shape, moved.dtype)] * SPAN,
        scratch_shapes=[
            pltpu.VMEM((TILE, HEAD_DIM), moved.dtype),
            pltpu.SemaphoreType.DMA((SPAN + 1,)),
        ],
        compiler_params=params(16),
        cost_estimate=pl.CostEstimate(flops=0, bytes_accessed=3 * 1024 * 1024, transcendentals=0),
        name="pack",
    )(moved)


def hidden(slots):
    page_len = slots.shape[2]
    row = lax.broadcasted_iota(jnp.int32, (page_len, HEAD_DIM), 0).astype(jnp.float32)
    parts = []
    for j in range(CAPK):
        tile = slots[j, 0, page_len - TILE :, 0:HEAD_DIM].astype(jnp.float32)
        flag = tile[TILE - 1 : TILE, 0:1]
        fill = jnp.where(flag > MARK - 1.0, flag - MARK, float(page_len))
        parts.append(jnp.where(row < fill, 0.0, MASKED))
    return jnp.concatenate(parts, axis=0)[:, 0:1]


def slot_rows(slots, which, cols):
    return [slots[j, which, :, cols] for j in range(CAPK)]


def finish_kernel(away_ref, proj_ref, sum_ref, top_ref, total_ref, read_ref, lead_ref, w_ref, *rest):
    pages, states = rest[: SPAN - 1], rest[SPAN - 1 : -4]
    out_ref, combined_ref, state_ref, sem = rest[-4:]
    away = away_ref[0]
    for i, state in enumerate(states):

        @pl.when(away == i)
        def _():
            pltpu.make_async_copy(state, state_ref, sem).start()

    hide = jnp.concatenate([hidden(slots) for slots in pages], axis=0)
    for h in range(HEADS):
        cols = slice(h * HEAD_DIM, (h + 1) * HEAD_DIM)
        keys = jnp.concatenate(sum((slot_rows(slots, 0, cols) for slots in pages), []), axis=0)
        values = jnp.concatenate(sum((slot_rows(slots, 1, cols) for slots in pages), []), axis=0)
        s = nt(keys, proj_ref[:, cols]) + hide
        before = top_ref[h : h + 1, :]
        top = jnp.maximum(before, s.max(axis=0, keepdims=True))
        p = jnp.exp2(s * SCALE2 - top * SCALE2)
        shrink = jnp.exp2((before - top) * SCALE2)
        total = total_ref[h : h + 1, :] * shrink + p.sum(axis=0, keepdims=True)
        gathered = sum_ref[cols, :] * shrink + nn(jnp.transpose(values), p.astype(jnp.bfloat16))
        attended = jnp.transpose(gathered * (1.0 / total))
        if h == 0:
            pltpu.make_async_copy(states[0], state_ref, sem).wait()
        reads = read_ref[:, cols] + nt(lead_ref[:, cols], state_ref[h])
        combined_ref[:, cols] = (attended + reads).astype(jnp.bfloat16)
    out_ref[...] = nn(combined_ref[...], w_ref[...]).astype(jnp.bfloat16)


def finish(away, projected, own_sum, top, total, reads, leads, w_out, pages, states):
    width, length = own_sum.shape
    return pl.pallas_call(
        finish_kernel,
        grid=(1,),
        in_specs=[SMEM, pl.BlockSpec((length, width), lambda i: (0, 0))]
        + [VMEM] * (6 + len(pages))
        + [ANY] * len(states),
        out_specs=VMEM,
        out_shape=jax.ShapeDtypeStruct((length, w_out.shape[1]), jnp.bfloat16),
        scratch_shapes=[
            pltpu.VMEM((length, width), jnp.bfloat16),
            pltpu.VMEM(states[0].shape, states[0].dtype),
            pltpu.SemaphoreType.DMA,
        ],
        compiler_params=params(40),
        cost_estimate=pl.CostEstimate(
            flops=2 * length * width * (w_out.shape[1] + 768),
            bytes_accessed=16 * length * width,
            transcendentals=length * 384 * HEADS,
        ),
        name="finish",
    )(away, projected, own_sum, top, total, reads, leads, w_out, *pages, *states)


def shifted(block, axis, distance):
    size = lax.axis_size(axis)
    return lax.ppermute(block, axis, [((i - distance) % size, i) for i in range(size)])


def exchanged(block, axis, bit):
    return lax.ppermute(block, axis, [(i ^ bit, i) for i in range(lax.axis_size(axis))])


def migrate(code, payload, beside, arrays):
    groups = lax.axis_size("req")
    orders = list(itertools.permutations(range(groups)))

    def branch(order):
        route = [(order[g], g) for g in range(groups)]
        return lambda x, *xs: (lax.ppermute(x, "req", route),) + tuple(beside(*xs))

    return lax.switch(code, [branch(order) for order in orders], payload, *arrays)


def on_device(
    tokens,
    norm_gain,
    w_qkv,
    w_out,
    w_gates,
    gate_bias,
    persistent,
    cache,
    page_back,
    page_fill,
    mem_state,
    mig_source,
):
    pages = cache.shape[2]
    rows = cache.reshape(-1, cache.shape[-1])
    payload, code, away = prepare(mig_source, page_back, page_fill, rows)
    moved, projected, gates, state = migrate(
        code[0], payload, project, (tokens[0, 0], norm_gain, w_qkv, jnp.transpose(w_gates), mem_state[0, 0])
    )
    near = exchanged(state, "req", 1)
    packed = pack_pages(moved, pages, cache.shape[3:])
    ahead = [shifted(packed[k], "seq", -k) for k in (4, 2, 3)]
    near, fifth, projected = lax.optimization_barrier((near, packed[5], projected))
    far = exchanged(jnp.where(away[1] == 1, near, state), "req", 2)
    ahead.append(shifted(fifth, "seq", -5))
    own_sum, top, total = own_attention(projected, persistent, packed[0])
    first, _ = lax.optimization_barrier((packed[1], top))
    arrived = [shifted(first, "seq", -1)] + ahead
    reads, leads = memory_reads(projected, gates, gate_bias)
    result = finish(
        away, projected, own_sum, top, total, reads, leads, w_out, arrived, (state, near, far)
    )
    return result[None, None]


def solution(mesh):
    return jax.shard_map(
        on_device,
        mesh=mesh,
        in_specs=(
            P("req", "seq", None, None),
            P(),
            P(),
            P(),
            P(),
            P(),
            P(),
            P("req", "seq", None, None, None, None),
            P("req", "seq", None),
            P("req", "seq", None),
            P("req", "seq", None, None, None),
            P("seq", None),
        ),
        out_specs=P("req", "seq", None, None),
        check_vma=False,
    )
```

```python
import itertools

import jax
import jax.numpy as jnp
from jax import lax
from jax.experimental import pallas as pl
from jax.experimental.pallas import tpu as pltpu
from jax.sharding import PartitionSpec as P

HEADS = 8
HEAD_DIM = 128
BLK = 64
SPAN = 6
CAPK = 2
LOG2E = 1.4426950408889634
SCALE2 = HEAD_DIM ** (-0.5) * LOG2E
MASKED = -1e30
MARK = 128.0
TILE = 16
TABLE = 8
CHUNK = 128
OUT_PARTS = 4
VMEM = pl.BlockSpec(memory_space=pltpu.VMEM)
SMEM = pl.BlockSpec(memory_space=pltpu.SMEM)
ANY = pl.BlockSpec(memory_space=pl.ANY)


def nt(a, b):
    return lax.dot_general(a, b, (((1,), (1,)), ((), ())), preferred_element_type=jnp.float32)


def nn(a, b):
    return lax.dot_general(a, b, (((1,), (0,)), ((), ())), preferred_element_type=jnp.float32)


def params(mib):
    return pltpu.CompilerParams(vmem_limit_bytes=mib * 1024 * 1024)


def project_kernel(
    tokens_ref, gain_ref, w_ref, wg_ref, state_ref, out_ref, gates_ref, rounded_ref, normed_ref
):
    length = tokens_ref.shape[0]

    def chunk(i):
        return pl.ds(pl.multiple_of(i * CHUNK, CHUNK), CHUNK)

    @pl.when(pl.program_id(0) == 0)
    def _():
        @pl.loop(0, length // CHUNK)
        def _(i):
            rows = tokens_ref[chunk(i), :].astype(jnp.float32)
            mean = jnp.mean(rows * rows, axis=-1, keepdims=True)
            normed = (rows * lax.rsqrt(mean + 1e-05) * gain_ref[...]).astype(jnp.bfloat16)
            normed_ref[chunk(i), :] = normed
            gates_ref[chunk(i), :] = nt(normed, wg_ref[...])

        @pl.loop(0, HEADS)
        def _(h):
            rounded_ref[h] = state_ref[h].astype(jnp.bfloat16)

    @pl.loop(0, length // CHUNK)
    def _(i):
        out_ref[chunk(i), :] = nn(normed_ref[chunk(i), :], w_ref[...]).astype(jnp.bfloat16)


def project(tokens, gain, w_qkv, gates_turned, state):
    length, width = tokens.shape
    columns = w_qkv.shape[1]
    tile = 512
    return pl.pallas_call(
        project_kernel,
        grid=(columns // tile,),
        in_specs=[
            pl.BlockSpec((length, width), lambda i: (0, 0)),
            pl.BlockSpec((1, width), lambda i: (0, 0)),
            pl.BlockSpec((width, tile), lambda i: (0, i)),
            pl.BlockSpec(gates_turned.shape, lambda i: (0, 0)),
            pl.BlockSpec(state.shape, lambda i: (0, 0, 0)),
        ],
        out_specs=[
            pl.BlockSpec((length, tile), lambda i: (0, i)),
            pl.BlockSpec((length, gates_turned.shape[0]), lambda i: (0, 0)),
            pl.BlockSpec(state.shape, lambda i: (0, 0, 0)),
        ],
        out_shape=[
            jax.ShapeDtypeStruct((length, columns), jnp.bfloat16),
            jax.ShapeDtypeStruct((length, gates_turned.shape[0]), jnp.float32),
            jax.ShapeDtypeStruct(state.shape, jnp.bfloat16),
        ],
        scratch_shapes=[pltpu.VMEM((length, width), jnp.bfloat16)],
        compiler_params=params(24),
        cost_estimate=pl.CostEstimate(
            flops=2 * length * width * columns,
            bytes_accessed=2 * (width * columns + length * width + length * columns),
            transcendentals=0,
        ),
        name="project",
    )(tokens, gain.reshape(1, width), w_qkv, gates_turned, state)


def own_kernel(proj_ref, lasting_ref, slots_ref, sum_ref, top_ref, total_ref):
    length = proj_ref.shape[0]
    width = HEADS * HEAD_DIM
    half = length // 2
    key = lax.broadcasted_iota(jnp.int32, (half, half), 0)
    token = lax.broadcasted_iota(jnp.int32, (half, half), 1)
    causal = key <= token
    hide = hidden(slots_ref)
    for h in range(HEADS):
        cols = slice(h * HEAD_DIM, (h + 1) * HEAD_DIM)
        keys = proj_ref[:, width + h * HEAD_DIM : width + (h + 1) * HEAD_DIM]
        page_keys = jnp.concatenate(slot_rows(slots_ref, 0, cols), axis=0)
        values = jnp.concatenate(
            slot_rows(slots_ref, 1, cols)
            + [
                lasting_ref[1, :, cols],
                proj_ref[:, 2 * width + h * HEAD_DIM : 2 * width + (h + 1) * HEAD_DIM],
            ],
            axis=0,
        )
        turned = jnp.transpose(values)
        for part in range(2):
            rows = slice(part * half, (part + 1) * half)
            q = proj_ref[rows, cols]
            scores = [nt(page_keys, q) + hide, nt(lasting_ref[0, :, cols], q)]
            scores += [nt(keys[i * half : (i + 1) * half], q) for i in range(part)]
            scores.append(jnp.where(causal, nt(keys[rows], q), MASKED))
            top = scores[1].max(axis=0, keepdims=True)
            for s in scores[:1] + scores[2:]:
                top = jnp.maximum(top, s.max(axis=0, keepdims=True))
            shift = top * SCALE2
            weights = [jnp.exp2(s * SCALE2 - shift) for s in scores]
            total = weights[0].sum(axis=0, keepdims=True)
            for w in weights[1:]:
                total = total + w.sum(axis=0, keepdims=True)
            rounded = jnp.concatenate([w.astype(jnp.bfloat16) for w in weights], axis=0)
            sum_ref[cols, rows] = nn(turned[:, : rounded.shape[0]], rounded)
            top_ref[h : h + 1, rows] = top
            total_ref[h : h + 1, rows] = total


def own_attention(projected, persistent, slots):
    length = projected.shape[0]
    width = HEADS * HEAD_DIM
    return pl.pallas_call(
        own_kernel,
        in_specs=[VMEM, VMEM, VMEM],
        out_specs=[VMEM, VMEM, VMEM],
        out_shape=[
            jax.ShapeDtypeStruct((width, length), jnp.float32),
            jax.ShapeDtypeStruct((HEADS, length), jnp.float32),
            jax.ShapeDtypeStruct((HEADS, length), jnp.float32),
        ],
        compiler_params=params(32),
        cost_estimate=pl.CostEstimate(
            flops=3 * length * length * width,
            bytes_accessed=10 * length * width,
            transcendentals=length * length * HEADS,
        ),
        name="own",
    )(projected, persistent, slots)


def memory_kernel(proj_ref, gates_ref, bias_ref, out_ref, lead_ref, mem_ref):
    length = proj_ref.shape[0]
    width = HEADS * HEAD_DIM
    blocks = length // BLK
    means = jnp.concatenate(
        [jnp.mean(gates_ref[b * BLK : (b + 1) * BLK, :], axis=0, keepdims=True) for b in range(blocks)],
        axis=0,
    )
    decay = 1.0 / (1.0 + jnp.exp(means[:, :HEADS] + bias_ref[0:1, :] - 2.5))
    rate = 0.5 / (1.0 + jnp.exp(-(means[:, HEADS : 2 * HEADS] + bias_ref[1:2, :])))
    mix = 1.0 / (1.0 + jnp.exp(-(gates_ref[:, 2 * HEADS :] + bias_ref[2:3, :])))
    one = lax.broadcasted_iota(jnp.int32, (HEAD_DIM, HEAD_DIM), 0) == lax.broadcasted_iota(
        jnp.int32, (HEAD_DIM, HEAD_DIM), 1
    )
    for b in range(blocks):
        rows = slice(b * BLK, (b + 1) * BLK)
        for h in range(HEADS):
            cols = slice(h * HEAD_DIM, (h + 1) * HEAD_DIM)
            q = proj_ref[rows, cols]
            k = proj_ref[rows, slice(width + h * HEAD_DIM, width + (h + 1) * HEAD_DIM)]
            v = proj_ref[rows, slice(2 * width + h * HEAD_DIM, 2 * width + (h + 1) * HEAD_DIM)]
            qf, kf = q.astype(jnp.float32), k.astype(jnp.float32)
            unit_q = lax.rsqrt(jnp.sum(qf * qf, axis=1, keepdims=True) + 1e-06) * mix[rows, h : h + 1]
            unit_k = lax.rsqrt(jnp.sum(kf * kf, axis=1, keepdims=True) + 1e-06)
            fade = decay[b : b + 1, h : h + 1]
            if b == 0:
                out_ref[rows, cols] = jnp.zeros((BLK, HEAD_DIM), jnp.float32)
                lead_ref[rows, cols] = (qf * unit_q).astype(jnp.bfloat16)
                held = kf * unit_k
                kept = jnp.concatenate(
                    [jnp.zeros((HEAD_DIM, HEAD_DIM), jnp.float32), jnp.where(one, fade, 0.0)], axis=1
                )
                error = jnp.concatenate([-v.astype(jnp.float32), held], axis=1)
            else:
                mem = mem_ref[h]
                both = nn(jnp.concatenate([q, k], axis=0), mem.astype(jnp.bfloat16))
                out_ref[rows, cols] = both[:BLK, :HEAD_DIM] * unit_q
                lead_ref[rows, cols] = (both[:BLK, HEAD_DIM:] * unit_q).astype(jnp.bfloat16)
                if b == blocks - 1:
                    continue
                kept = mem * fade
                error = jnp.concatenate(
                    [
                        both[BLK:, :HEAD_DIM] * unit_k - v.astype(jnp.float32),
                        both[BLK:, HEAD_DIM:] * unit_k,
                    ],
                    axis=1,
                )
            step = error * (unit_k * -rate[b : b + 1, h : h + 1])
            mem_ref[h] = kept + nn(jnp.transpose(kf).astype(jnp.bfloat16), step.astype(jnp.bfloat16))


def memory_reads(projected, gates, gate_bias):
    length = projected.shape[0]
    width = HEADS * HEAD_DIM
    return pl.pallas_call(
        memory_kernel,
        in_specs=[VMEM] * 3,
        out_specs=[VMEM] * 2,
        out_shape=[
            jax.ShapeDtypeStruct((length, width), jnp.float32),
            jax.ShapeDtypeStruct((length, width), jnp.bfloat16),
        ],
        scratch_shapes=[pltpu.VMEM((HEADS, HEAD_DIM, 2 * HEAD_DIM), jnp.float32)],
        compiler_params=params(32),
        cost_estimate=pl.CostEstimate(
            flops=12 * length * HEAD_DIM * width,
            bytes_accessed=12 * length * width,
            transcendentals=0,
        ),
        name="memory",
    )(projected, gates, gate_bias)


def prepare_kernel(
    sources_ref, back_ref, fill_ref, cache_ref, out_ref, code_ref, away_ref, relay_ref,
    order_ref, place_ref, used_ref, where_ref, count_ref, held_ref, sem,
):
    cached = cache_ref.shape[0]
    pages = back_ref.shape[2]
    page_rows = cached // pages
    page_len = page_rows // 2
    groups = sources_ref.shape[1]
    whole = pltpu.make_async_copy(cache_ref, held_ref.at[pl.ds(0, cached)], sem.at[3])
    whole.start()
    loads = [
        pltpu.make_async_copy(sources_ref, order_ref, sem.at[0]),
        pltpu.make_async_copy(back_ref.at[0], place_ref, sem.at[1]),
        pltpu.make_async_copy(fill_ref.at[0], used_ref, sem.at[2]),
    ]
    for load in loads:
        load.start()
    for slot in range(SPAN * CAPK):
        where_ref[slot] = pages
    for distance in range(SPAN):
        count_ref[distance] = 0
    for load in loads:
        load.wait()
    code = jnp.int32(0)
    for g in range(groups - 1):
        smaller = jnp.int32(0)
        for later in range(g + 1, groups):
            smaller = smaller + (order_ref[0, later] < order_ref[0, g]).astype(jnp.int32)
        code = code * (groups - g) + smaller
    code_ref[0] = code
    here = lax.axis_index("req")
    source, near = order_ref[0, here], here ^ 1
    away_ref[0] = jnp.where(source == here, 0, jnp.where(source == near, 1, 2))
    relay_ref[0] = (order_ref[0, here ^ 2] == near).astype(jnp.int32)
    for page in range(pages):
        distance = place_ref[0, page]
        taken = count_ref[distance]
        where_ref[distance * CAPK + taken] = page
        count_ref[distance] = taken + 1
    lane = lax.broadcasted_iota(jnp.int32, (TABLE, HEAD_DIM), 1)
    row = lax.broadcasted_iota(jnp.int32, (TILE, HEAD_DIM), 0)
    line = jnp.zeros((TABLE, HEAD_DIM), jnp.float32)
    for distance in range(SPAN):
        entry = where_ref[distance * CAPK] * 16 + where_ref[distance * CAPK + 1]
        line = jnp.where(lane == distance, entry.astype(jnp.float32), line)
    held_ref[cached:, :] = jnp.zeros((TABLE, held_ref.shape[1]), jnp.bfloat16)
    held_ref[cached:, 0:HEAD_DIM] = line.astype(jnp.bfloat16)
    whole.wait()
    for page in range(pages):
        fill = used_ref[0, page]
        last = slice(page * page_rows + page_len - TILE, page * page_rows + page_len)
        marked = jnp.where(
            (row == TILE - 1) & (fill < page_len),
            MARK + fill.astype(jnp.float32),
            held_ref[last, 0:HEAD_DIM].astype(jnp.float32),
        )
        held_ref[last, 0:HEAD_DIM] = marked.astype(jnp.bfloat16)
    store = pltpu.make_async_copy(held_ref, out_ref, sem.at[4])
    store.start()
    store.wait()


def prepare(sources, back, fill, cache):
    cached, width = cache.shape
    pages = back.shape[2]
    return pl.pallas_call(
        prepare_kernel,
        in_specs=[ANY] * 4,
        out_specs=[ANY, SMEM, SMEM, SMEM],
        out_shape=[
            jax.ShapeDtypeStruct((cached + TABLE, width), cache.dtype),
            jax.ShapeDtypeStruct((1,), jnp.int32),
            jax.ShapeDtypeStruct((1,), jnp.int32),
            jax.ShapeDtypeStruct((1,), jnp.int32),
        ],
        scratch_shapes=[
            pltpu.SMEM(sources.shape, jnp.int32),
            pltpu.SMEM((1, pages), jnp.int32),
            pltpu.SMEM((1, pages), jnp.int32),
            pltpu.SMEM((SPAN * CAPK,), jnp.int32),
            pltpu.SMEM((SPAN,), jnp.int32),
            pltpu.VMEM((cached + TABLE, width), cache.dtype),
            pltpu.SemaphoreType.DMA((5,)),
        ],
        compiler_params=params(56),
        cost_estimate=pl.CostEstimate(flops=0, bytes_accessed=2 * 1024 * 1024, transcendentals=0),
        name="prepare",
    )(sources, back, fill, cache)


def pack_kernel(moved_ref, *rest):
    outs = rest[:SPAN]
    line_ref, sem = rest[SPAN:]
    page_len = outs[0].shape[2]
    page_rows = 2 * page_len
    cached = moved_ref.shape[0] - TABLE
    pages = cached // page_rows
    table = pltpu.make_async_copy(
        moved_ref.at[pl.ds(cached, TABLE), pl.ds(0, HEAD_DIM)], line_ref, sem.at[SPAN]
    )
    table.start()
    table.wait()
    line = line_ref[...].astype(jnp.float32)
    lane = lax.broadcasted_iota(jnp.int32, line.shape, 1)
    entries = [
        jnp.max(jnp.where(lane == distance, line, 0.0)).astype(jnp.int32) for distance in range(SPAN)
    ]
    for distance in range(SPAN):
        for j, page in enumerate((entries[distance] >> 4, entries[distance] & 15)):

            @pl.when(page < pages)
            def _():
                for half in range(2):
                    start = pl.multiple_of(page * page_rows + half * page_len, page_len)
                    pltpu.make_async_copy(
                        moved_ref.at[pl.ds(start, page_len)], outs[distance].at[j, half], sem.at[distance]
                    ).start()

            @pl.when(page >= pages)
            def _():
                outs[distance][j] = jnp.zeros(outs[distance].shape[1:], moved_ref.dtype)
                outs[distance][j, 0, page_len - TILE :, 0:HEAD_DIM] = jnp.full(
                    (TILE, HEAD_DIM), MARK, moved_ref.dtype
                )

    for distance in range(SPAN):
        for j, page in enumerate((entries[distance] >> 4, entries[distance] & 15)):

            @pl.when(page < pages)
            def _():
                for half in range(2):
                    pltpu.make_async_copy(
                        moved_ref.at[pl.ds(0, page_len)], outs[distance].at[j, half], sem.at[distance]
                    ).wait()


def pack_pages(moved, pages, page_shape):
    shape = (CAPK,) + page_shape
    return pl.pallas_call(
        pack_kernel,
        in_specs=[ANY],
        out_specs=[VMEM] * SPAN,
        out_shape=[jax.ShapeDtypeStruct(shape, moved.dtype)] * SPAN,
        scratch_shapes=[
            pltpu.VMEM((TABLE, HEAD_DIM), moved.dtype),
            pltpu.SemaphoreType.DMA((SPAN + 1,)),
        ],
        compiler_params=params(16),
        cost_estimate=pl.CostEstimate(flops=0, bytes_accessed=3 * 1024 * 1024, transcendentals=0),
        name="pack",
    )(moved)


def hidden(slots):
    page_len = slots.shape[2]
    row = lax.broadcasted_iota(jnp.int32, (page_len, HEAD_DIM), 0).astype(jnp.float32)
    parts = []
    for j in range(CAPK):
        tile = slots[j, 0, page_len - TILE :, 0:HEAD_DIM].astype(jnp.float32)
        flag = tile[TILE - 1 : TILE, 0:1]
        fill = jnp.where(flag > MARK - 1.0, flag - MARK, float(page_len))
        parts.append(jnp.where(row < fill, 0.0, MASKED))
    return jnp.concatenate(parts, axis=0)[:, 0:1]


def slot_rows(slots, which, cols):
    return [slots[j, which, :, cols] for j in range(CAPK)]


def finish_kernel(away_ref, proj_ref, sum_ref, top_ref, total_ref, read_ref, lead_ref, w_ref, *rest):
    pages, states = rest[: SPAN - 1], rest[SPAN - 1 : -6]
    out_ref, combined_ref, state_ref, result_ref, sem, out_sem = rest[-6:]
    away = away_ref[0]
    for i, state in enumerate(states):

        @pl.when(away == i)
        def _():
            pltpu.make_async_copy(state, state_ref, sem).start()

    hide = jnp.concatenate([hidden(slots) for slots in pages], axis=0)
    for h in range(HEADS):
        cols = slice(h * HEAD_DIM, (h + 1) * HEAD_DIM)
        keys = jnp.concatenate(sum((slot_rows(slots, 0, cols) for slots in pages), []), axis=0)
        values = jnp.concatenate(sum((slot_rows(slots, 1, cols) for slots in pages), []), axis=0)
        s = nt(keys, proj_ref[:, cols]) + hide
        before = top_ref[h : h + 1, :]
        top = jnp.maximum(before, s.max(axis=0, keepdims=True))
        p = jnp.exp2(s * SCALE2 - top * SCALE2)
        shrink = jnp.exp2((before - top) * SCALE2)
        total = total_ref[h : h + 1, :] * shrink + p.sum(axis=0, keepdims=True)
        gathered = sum_ref[cols, :] * shrink + nn(jnp.transpose(values), p.astype(jnp.bfloat16))
        if h == 0:
            pltpu.make_async_copy(states[0], state_ref, sem).wait()
        turned = gathered * (1.0 / total) + nt(state_ref[h], lead_ref[:, cols])
        combined_ref[:, cols] = (jnp.transpose(turned) + read_ref[:, cols]).astype(jnp.bfloat16)
    stores = []
    for i in range(OUT_PARTS):
        part = out_ref.shape[0] // OUT_PARTS
        rows = slice(i * part, (i + 1) * part)
        result_ref[rows, :] = nn(combined_ref[rows, :], w_ref[...]).astype(jnp.bfloat16)
        stores.append(pltpu.make_async_copy(result_ref.at[rows], out_ref.at[rows], out_sem.at[i]))
        stores[-1].start()
    for store in stores:
        store.wait()


def finish(away, projected, own_sum, top, total, reads, leads, w_out, pages, states):
    width, length = own_sum.shape
    return pl.pallas_call(
        finish_kernel,
        in_specs=[SMEM]
        + [VMEM] * (7 + len(pages))
        + [ANY] * len(states),
        out_specs=ANY,
        out_shape=jax.ShapeDtypeStruct((length, w_out.shape[1]), jnp.bfloat16),
        scratch_shapes=[
            pltpu.VMEM((length, width), jnp.bfloat16),
            pltpu.VMEM(states[0].shape, states[0].dtype),
            pltpu.VMEM((length, w_out.shape[1]), jnp.bfloat16),
            pltpu.SemaphoreType.DMA,
            pltpu.SemaphoreType.DMA((OUT_PARTS,)),
        ],
        compiler_params=params(40),
        cost_estimate=pl.CostEstimate(
            flops=2 * length * width * (w_out.shape[1] + 768),
            bytes_accessed=16 * length * width,
            transcendentals=length * 384 * HEADS,
        ),
        name="finish",
    )(away, projected, own_sum, top, total, reads, leads, w_out, *pages, *states)


def shifted(block, axis, distance):
    size = lax.axis_size(axis)
    return lax.ppermute(block, axis, [((i - distance) % size, i) for i in range(size)])


def exchanged(block, axis, bit):
    return lax.ppermute(block, axis, [(i ^ bit, i) for i in range(lax.axis_size(axis))])


def migrate(code, payload, beside, arrays):
    groups = lax.axis_size("req")
    orders = list(itertools.permutations(range(groups)))

    def branch(order):
        route = [(order[g], g) for g in range(groups)]
        return lambda x, *xs: (lax.ppermute(x, "req", route),) + tuple(beside(*xs))

    return lax.switch(code, [branch(order) for order in orders], payload, *arrays)


def on_device(
    tokens,
    norm_gain,
    w_qkv,
    w_out,
    w_gates,
    gate_bias,
    persistent,
    cache,
    page_back,
    page_fill,
    mem_state,
    mig_source,
):
    pages = cache.shape[2]
    rows = cache.reshape(-1, cache.shape[-1])
    payload, code, away, relay = prepare(mig_source, page_back, page_fill, rows)
    moved, projected, gates, state = migrate(
        code[0], payload, project, (tokens[0, 0], norm_gain, w_qkv, jnp.transpose(w_gates), mem_state[0, 0])
    )
    near = exchanged(state, "req", 1)
    packed = pack_pages(moved, pages, cache.shape[3:])
    ahead = [shifted(packed[k], "seq", -k) for k in (4, 2, 3)]
    near, fifth, projected = lax.optimization_barrier((near, packed[5], projected))
    far = exchanged(jnp.where(relay[0] == 1, near, state), "req", 2)
    ahead.append(shifted(fifth, "seq", -5))
    own_sum, top, total = own_attention(projected, persistent, packed[0])
    first, _ = lax.optimization_barrier((packed[1], top))
    arrived = [shifted(first, "seq", -1)] + ahead
    reads, leads = memory_reads(projected, gates, gate_bias)
    result = finish(
        away, projected, own_sum, top, total, reads, leads, w_out, arrived, (state, near, far)
    )
    return result[None, None]


def solution(mesh):
    return jax.shard_map(
        on_device,
        mesh=mesh,
        in_specs=(
            P("req", "seq", None, None),
            P(),
            P(),
            P(),
            P(),
            P(),
            P(),
            P("req", "seq", None, None, None, None),
            P("req", "seq", None),
            P("req", "seq", None),
            P("req", "seq", None, None, None),
            P("seq", None),
        ),
        out_specs=P("req", "seq", None, None),
        check_vma=False,
    )
```

```python
import itertools

import jax
import jax.numpy as jnp
from jax import lax
from jax.experimental import pallas as pl
from jax.experimental.pallas import tpu as pltpu
from jax.sharding import PartitionSpec as P

HEADS = 8
HEAD_DIM = 128
BLK = 64
SPAN = 6
CAPK = 2
LOG2E = 1.4426950408889634
SCALE2 = HEAD_DIM ** (-0.5) * LOG2E
MASKED = -1e30
MARK = 128.0
TILE = 16
TABLE = 8
CHUNK = 128
OUT_PARTS = 4
VMEM = pl.BlockSpec(memory_space=pltpu.VMEM)
SMEM = pl.BlockSpec(memory_space=pltpu.SMEM)
ANY = pl.BlockSpec(memory_space=pl.ANY)


def nt(a, b):
    return lax.dot_general(a, b, (((1,), (1,)), ((), ())), preferred_element_type=jnp.float32)


def nn(a, b):
    return lax.dot_general(a, b, (((1,), (0,)), ((), ())), preferred_element_type=jnp.float32)


def params(mib):
    return pltpu.CompilerParams(vmem_limit_bytes=mib * 1024 * 1024)


def project_kernel(
    tokens_ref, gain_ref, w_ref, wg_ref, state_ref, out_ref, gates_ref, rounded_ref, normed_ref
):
    length = tokens_ref.shape[0]

    def chunk(i):
        return pl.ds(pl.multiple_of(i * CHUNK, CHUNK), CHUNK)

    @pl.when(pl.program_id(0) == 0)
    def _():
        @pl.loop(0, length // CHUNK)
        def _(i):
            rows = tokens_ref[chunk(i), :].astype(jnp.float32)
            mean = jnp.mean(rows * rows, axis=-1, keepdims=True)
            normed = (rows * lax.rsqrt(mean + 1e-05) * gain_ref[...]).astype(jnp.bfloat16)
            normed_ref[chunk(i), :] = normed
            gates_ref[chunk(i), :] = nt(normed, wg_ref[...])

        @pl.loop(0, HEADS)
        def _(h):
            rounded_ref[h] = state_ref[h].astype(jnp.bfloat16)

    @pl.loop(0, length // CHUNK)
    def _(i):
        out_ref[chunk(i), :] = nn(normed_ref[chunk(i), :], w_ref[...]).astype(jnp.bfloat16)


def project(tokens, gain, w_qkv, gates_turned, state):
    length, width = tokens.shape
    columns = w_qkv.shape[1]
    tile = 512
    return pl.pallas_call(
        project_kernel,
        grid=(columns // tile,),
        in_specs=[
            pl.BlockSpec((length, width), lambda i: (0, 0)),
            pl.BlockSpec((1, width), lambda i: (0, 0)),
            pl.BlockSpec((width, tile), lambda i: (0, i)),
            pl.BlockSpec(gates_turned.shape, lambda i: (0, 0)),
            pl.BlockSpec(state.shape, lambda i: (0, 0, 0)),
        ],
        out_specs=[
            pl.BlockSpec((length, tile), lambda i: (0, i)),
            pl.BlockSpec((length, gates_turned.shape[0]), lambda i: (0, 0)),
            pl.BlockSpec(state.shape, lambda i: (0, 0, 0)),
        ],
        out_shape=[
            jax.ShapeDtypeStruct((length, columns), jnp.bfloat16),
            jax.ShapeDtypeStruct((length, gates_turned.shape[0]), jnp.float32),
            jax.ShapeDtypeStruct(state.shape, jnp.bfloat16),
        ],
        scratch_shapes=[pltpu.VMEM((length, width), jnp.bfloat16)],
        compiler_params=params(24),
        cost_estimate=pl.CostEstimate(
            flops=2 * length * width * columns,
            bytes_accessed=2 * (width * columns + length * width + length * columns),
            transcendentals=0,
        ),
        name="project",
    )(tokens, gain.reshape(1, width), w_qkv, gates_turned, state)


def own_kernel(proj_ref, lasting_ref, slots_ref, sum_ref, top_ref, total_ref):
    length = proj_ref.shape[0]
    width = HEADS * HEAD_DIM
    half = length // 2
    key = lax.broadcasted_iota(jnp.int32, (half, half), 0)
    token = lax.broadcasted_iota(jnp.int32, (half, half), 1)
    causal = key <= token
    hide = hidden(slots_ref)
    for h in range(HEADS):
        cols = slice(h * HEAD_DIM, (h + 1) * HEAD_DIM)
        keys = proj_ref[:, width + h * HEAD_DIM : width + (h + 1) * HEAD_DIM]
        page_keys = jnp.concatenate(slot_rows(slots_ref, 0, cols), axis=0)
        values = jnp.concatenate(
            slot_rows(slots_ref, 1, cols)
            + [
                lasting_ref[1, :, cols],
                proj_ref[:, 2 * width + h * HEAD_DIM : 2 * width + (h + 1) * HEAD_DIM],
            ],
            axis=0,
        )
        turned = jnp.transpose(values)
        for part in range(2):
            rows = slice(part * half, (part + 1) * half)
            q = proj_ref[rows, cols]
            scores = [nt(page_keys, q) + hide, nt(lasting_ref[0, :, cols], q)]
            scores += [nt(keys[i * half : (i + 1) * half], q) for i in range(part)]
            scores.append(jnp.where(causal, nt(keys[rows], q), MASKED))
            top = scores[1].max(axis=0, keepdims=True)
            for s in scores[:1] + scores[2:]:
                top = jnp.maximum(top, s.max(axis=0, keepdims=True))
            shift = top * SCALE2
            weights = [jnp.exp2(s * SCALE2 - shift) for s in scores]
            total = weights[0].sum(axis=0, keepdims=True)
            for w in weights[1:]:
                total = total + w.sum(axis=0, keepdims=True)
            rounded = jnp.concatenate([w.astype(jnp.bfloat16) for w in weights], axis=0)
            sum_ref[cols, rows] = nn(turned[:, : rounded.shape[0]], rounded)
            top_ref[h : h + 1, rows] = top
            total_ref[h : h + 1, rows] = total


def own_attention(projected, persistent, slots):
    length = projected.shape[0]
    width = HEADS * HEAD_DIM
    return pl.pallas_call(
        own_kernel,
        in_specs=[VMEM, VMEM, VMEM],
        out_specs=[VMEM, VMEM, VMEM],
        out_shape=[
            jax.ShapeDtypeStruct((width, length), jnp.float32),
            jax.ShapeDtypeStruct((HEADS, length), jnp.float32),
            jax.ShapeDtypeStruct((HEADS, length), jnp.float32),
        ],
        compiler_params=params(32),
        cost_estimate=pl.CostEstimate(
            flops=3 * length * length * width,
            bytes_accessed=10 * length * width,
            transcendentals=length * length * HEADS,
        ),
        name="own",
    )(projected, persistent, slots)


def memory_kernel(proj_ref, gates_ref, bias_ref, out_ref, lead_ref, mem_ref):
    length = proj_ref.shape[0]
    width = HEADS * HEAD_DIM
    blocks = length // BLK
    means = jnp.concatenate(
        [jnp.mean(gates_ref[b * BLK : (b + 1) * BLK, :], axis=0, keepdims=True) for b in range(blocks)],
        axis=0,
    )
    decay = 1.0 / (1.0 + jnp.exp(means[:, :HEADS] + bias_ref[0:1, :] - 2.5))
    rate = 0.5 / (1.0 + jnp.exp(-(means[:, HEADS : 2 * HEADS] + bias_ref[1:2, :])))
    mix = 1.0 / (1.0 + jnp.exp(-(gates_ref[:, 2 * HEADS :] + bias_ref[2:3, :])))
    one = lax.broadcasted_iota(jnp.int32, (HEAD_DIM, HEAD_DIM), 0) == lax.broadcasted_iota(
        jnp.int32, (HEAD_DIM, HEAD_DIM), 1
    )
    for b in range(blocks):
        rows = slice(b * BLK, (b + 1) * BLK)
        for h in range(HEADS):
            cols = slice(h * HEAD_DIM, (h + 1) * HEAD_DIM)
            q = proj_ref[rows, cols]
            k = proj_ref[rows, slice(width + h * HEAD_DIM, width + (h + 1) * HEAD_DIM)]
            v = proj_ref[rows, slice(2 * width + h * HEAD_DIM, 2 * width + (h + 1) * HEAD_DIM)]
            qf, kf = q.astype(jnp.float32), k.astype(jnp.float32)
            unit_q = lax.rsqrt(jnp.sum(qf * qf, axis=1, keepdims=True) + 1e-06) * mix[rows, h : h + 1]
            unit_k = lax.rsqrt(jnp.sum(kf * kf, axis=1, keepdims=True) + 1e-06)
            fade = decay[b : b + 1, h : h + 1]
            if b == 0:
                out_ref[rows, cols] = jnp.zeros((BLK, HEAD_DIM), jnp.float32)
                lead_ref[rows, cols] = (qf * unit_q).astype(jnp.bfloat16)
                held = kf * unit_k
                kept = jnp.concatenate(
                    [jnp.zeros((HEAD_DIM, HEAD_DIM), jnp.float32), jnp.where(one, fade, 0.0)], axis=1
                )
                error = jnp.concatenate([-v.astype(jnp.float32), held], axis=1)
            else:
                mem = mem_ref[h]
                both = nn(jnp.concatenate([q, k], axis=0), mem.astype(jnp.bfloat16))
                out_ref[rows, cols] = both[:BLK, :HEAD_DIM] * unit_q
                lead_ref[rows, cols] = (both[:BLK, HEAD_DIM:] * unit_q).astype(jnp.bfloat16)
                if b == blocks - 1:
                    continue
                kept = mem * fade
                error = jnp.concatenate(
                    [
                        both[BLK:, :HEAD_DIM] * unit_k - v.astype(jnp.float32),
                        both[BLK:, HEAD_DIM:] * unit_k,
                    ],
                    axis=1,
                )
            step = error * (unit_k * -rate[b : b + 1, h : h + 1])
            mem_ref[h] = kept + nn(jnp.transpose(kf).astype(jnp.bfloat16), step.astype(jnp.bfloat16))


def memory_reads(projected, gates, gate_bias):
    length = projected.shape[0]
    width = HEADS * HEAD_DIM
    return pl.pallas_call(
        memory_kernel,
        in_specs=[VMEM] * 3,
        out_specs=[VMEM] * 2,
        out_shape=[
            jax.ShapeDtypeStruct((length, width), jnp.float32),
            jax.ShapeDtypeStruct((length, width), jnp.bfloat16),
        ],
        scratch_shapes=[pltpu.VMEM((HEADS, HEAD_DIM, 2 * HEAD_DIM), jnp.float32)],
        compiler_params=params(32),
        cost_estimate=pl.CostEstimate(
            flops=12 * length * HEAD_DIM * width,
            bytes_accessed=12 * length * width,
            transcendentals=0,
        ),
        name="memory",
    )(projected, gates, gate_bias)


def prepare_kernel(
    sources_ref, back_ref, fill_ref, cache_ref, out_ref, code_ref, away_ref, relay_ref,
    order_ref, place_ref, used_ref, where_ref, count_ref, held_ref, sem,
):
    cached = cache_ref.shape[0]
    pages = back_ref.shape[2]
    page_rows = cached // pages
    page_len = page_rows // 2
    groups = sources_ref.shape[1]
    whole = pltpu.make_async_copy(cache_ref, held_ref.at[pl.ds(0, cached)], sem.at[3])
    whole.start()
    loads = [
        pltpu.make_async_copy(sources_ref, order_ref, sem.at[0]),
        pltpu.make_async_copy(back_ref.at[0], place_ref, sem.at[1]),
        pltpu.make_async_copy(fill_ref.at[0], used_ref, sem.at[2]),
    ]
    for load in loads:
        load.start()
    for slot in range(SPAN * CAPK):
        where_ref[slot] = pages
    for distance in range(SPAN):
        count_ref[distance] = 0
    for load in loads:
        load.wait()
    code = jnp.int32(0)
    for g in range(groups - 1):
        smaller = jnp.int32(0)
        for later in range(g + 1, groups):
            smaller = smaller + (order_ref[0, later] < order_ref[0, g]).astype(jnp.int32)
        code = code * (groups - g) + smaller
    code_ref[0] = code
    here = lax.axis_index("req")
    source, near = order_ref[0, here], here ^ 1
    away_ref[0] = jnp.where(source == here, 0, jnp.where(source == near, 1, 2))
    relay_ref[0] = (order_ref[0, here ^ 2] == near).astype(jnp.int32)
    for page in range(pages):
        distance = place_ref[0, page]
        taken = count_ref[distance]
        where_ref[distance * CAPK + taken] = page
        count_ref[distance] = taken + 1
    lane = lax.broadcasted_iota(jnp.int32, (TABLE, HEAD_DIM), 1)
    row = lax.broadcasted_iota(jnp.int32, (TILE, HEAD_DIM), 0)
    line = jnp.zeros((TABLE, HEAD_DIM), jnp.float32)
    for distance in range(SPAN):
        entry = where_ref[distance * CAPK] * 16 + where_ref[distance * CAPK + 1]
        line = jnp.where(lane == distance, entry.astype(jnp.float32), line)
    held_ref[cached:, :] = jnp.zeros((TABLE, held_ref.shape[1]), jnp.bfloat16)
    held_ref[cached:, 0:HEAD_DIM] = line.astype(jnp.bfloat16)
    whole.wait()
    for page in range(pages):
        fill = used_ref[0, page]
        last = slice(page * page_rows + page_len - TILE, page * page_rows + page_len)
        marked = jnp.where(
            (row == TILE - 1) & (fill < page_len),
            MARK + fill.astype(jnp.float32),
            held_ref[last, 0:HEAD_DIM].astype(jnp.float32),
        )
        held_ref[last, 0:HEAD_DIM] = marked.astype(jnp.bfloat16)
    store = pltpu.make_async_copy(held_ref, out_ref, sem.at[4])
    store.start()
    store.wait()


def prepare(sources, back, fill, cache):
    cached, width = cache.shape
    pages = back.shape[2]
    return pl.pallas_call(
        prepare_kernel,
        in_specs=[ANY] * 4,
        out_specs=[ANY, SMEM, SMEM, SMEM],
        out_shape=[
            jax.ShapeDtypeStruct((cached + TABLE, width), cache.dtype),
            jax.ShapeDtypeStruct((1,), jnp.int32),
            jax.ShapeDtypeStruct((1,), jnp.int32),
            jax.ShapeDtypeStruct((1,), jnp.int32),
        ],
        scratch_shapes=[
            pltpu.SMEM(sources.shape, jnp.int32),
            pltpu.SMEM((1, pages), jnp.int32),
            pltpu.SMEM((1, pages), jnp.int32),
            pltpu.SMEM((SPAN * CAPK,), jnp.int32),
            pltpu.SMEM((SPAN,), jnp.int32),
            pltpu.VMEM((cached + TABLE, width), cache.dtype),
            pltpu.SemaphoreType.DMA((5,)),
        ],
        compiler_params=params(56),
        cost_estimate=pl.CostEstimate(flops=0, bytes_accessed=2 * 1024 * 1024, transcendentals=0),
        name="prepare",
    )(sources, back, fill, cache)


def pack_kernel(moved_ref, *rest):
    outs = rest[:SPAN]
    line_ref, sem = rest[SPAN:]
    page_len = outs[0].shape[2]
    page_rows = 2 * page_len
    cached = moved_ref.shape[0] - TABLE
    pages = cached // page_rows
    table = pltpu.make_async_copy(
        moved_ref.at[pl.ds(cached, TABLE), pl.ds(0, HEAD_DIM)], line_ref, sem.at[SPAN]
    )
    table.start()
    table.wait()
    line = line_ref[...].astype(jnp.float32)
    lane = lax.broadcasted_iota(jnp.int32, line.shape, 1)
    entries = [
        jnp.max(jnp.where(lane == distance, line, 0.0)).astype(jnp.int32) for distance in range(SPAN)
    ]
    for distance in range(SPAN):
        for j, page in enumerate((entries[distance] >> 4, entries[distance] & 15)):

            @pl.when(page < pages)
            def _():
                for half in range(2):
                    start = pl.multiple_of(page * page_rows + half * page_len, page_len)
                    pltpu.make_async_copy(
                        moved_ref.at[pl.ds(start, page_len)], outs[distance].at[j, half], sem.at[distance]
                    ).start()

            @pl.when(page >= pages)
            def _():
                outs[distance][j] = jnp.zeros(outs[distance].shape[1:], moved_ref.dtype)
                outs[distance][j, 0, page_len - TILE :, 0:HEAD_DIM] = jnp.full(
                    (TILE, HEAD_DIM), MARK, moved_ref.dtype
                )

    for distance in range(SPAN):
        for j, page in enumerate((entries[distance] >> 4, entries[distance] & 15)):

            @pl.when(page < pages)
            def _():
                for half in range(2):
                    pltpu.make_async_copy(
                        moved_ref.at[pl.ds(0, page_len)], outs[distance].at[j, half], sem.at[distance]
                    ).wait()


def pack_pages(moved, pages, page_shape):
    shape = (CAPK,) + page_shape
    return pl.pallas_call(
        pack_kernel,
        in_specs=[ANY],
        out_specs=[VMEM] * SPAN,
        out_shape=[jax.ShapeDtypeStruct(shape, moved.dtype)] * SPAN,
        scratch_shapes=[
            pltpu.VMEM((TABLE, HEAD_DIM), moved.dtype),
            pltpu.SemaphoreType.DMA((SPAN + 1,)),
        ],
        compiler_params=params(16),
        cost_estimate=pl.CostEstimate(flops=0, bytes_accessed=3 * 1024 * 1024, transcendentals=0),
        name="pack",
    )(moved)


def hidden(slots):
    page_len = slots.shape[2]
    row = lax.broadcasted_iota(jnp.int32, (page_len, HEAD_DIM), 0).astype(jnp.float32)
    parts = []
    for j in range(CAPK):
        tile = slots[j, 0, page_len - TILE :, 0:HEAD_DIM].astype(jnp.float32)
        flag = tile[TILE - 1 : TILE, 0:1]
        fill = jnp.where(flag > MARK - 1.0, flag - MARK, float(page_len))
        parts.append(jnp.where(row < fill, 0.0, MASKED))
    return jnp.concatenate(parts, axis=0)[:, 0:1]


def slot_rows(slots, which, cols):
    return [slots[j, which, :, cols] for j in range(CAPK)]


def finish_kernel(away_ref, proj_ref, sum_ref, top_ref, total_ref, read_ref, lead_ref, w_ref, *rest):
    pages, states = rest[: SPAN - 1], rest[SPAN - 1 : -6]
    out_ref, combined_ref, state_ref, result_ref, sem, out_sem = rest[-6:]
    away = away_ref[0]
    for i, state in enumerate(states):

        @pl.when(away == i)
        def _():
            pltpu.make_async_copy(state, state_ref, sem).start()

    hide = jnp.concatenate([hidden(slots) for slots in pages], axis=0)
    for h in range(HEADS):
        cols = slice(h * HEAD_DIM, (h + 1) * HEAD_DIM)
        keys = jnp.concatenate(sum((slot_rows(slots, 0, cols) for slots in pages), []), axis=0)
        values = jnp.concatenate(sum((slot_rows(slots, 1, cols) for slots in pages), []), axis=0)
        s = nt(keys, proj_ref[:, cols]) + hide
        before = top_ref[h : h + 1, :]
        top = jnp.maximum(before, s.max(axis=0, keepdims=True))
        p = jnp.exp2(s * SCALE2 - top * SCALE2)
        shrink = jnp.exp2((before - top) * SCALE2)
        total = total_ref[h : h + 1, :] * shrink + p.sum(axis=0, keepdims=True)
        gathered = sum_ref[cols, :] * shrink + nn(jnp.transpose(values), p.astype(jnp.bfloat16))
        if h == 0:
            pltpu.make_async_copy(states[0], state_ref, sem).wait()
        turned = gathered * (1.0 / total) + nt(state_ref[h], lead_ref[:, cols])
        combined_ref[:, cols] = (jnp.transpose(turned) + read_ref[:, cols]).astype(jnp.bfloat16)
    stores = []
    for i in range(OUT_PARTS):
        part = out_ref.shape[0] // OUT_PARTS
        rows = slice(i * part, (i + 1) * part)
        result_ref[rows, :] = nn(combined_ref[rows, :], w_ref[...]).astype(jnp.bfloat16)
        stores.append(pltpu.make_async_copy(result_ref.at[rows], out_ref.at[rows], out_sem.at[i]))
        stores[-1].start()
    for store in stores:
        store.wait()


def finish(away, projected, own_sum, top, total, reads, leads, w_out, pages, states):
    width, length = own_sum.shape
    return pl.pallas_call(
        finish_kernel,
        in_specs=[SMEM]
        + [VMEM] * (7 + len(pages))
        + [ANY] * len(states),
        out_specs=ANY,
        out_shape=jax.ShapeDtypeStruct((length, w_out.shape[1]), jnp.bfloat16),
        scratch_shapes=[
            pltpu.VMEM((length, width), jnp.bfloat16),
            pltpu.VMEM(states[0].shape, states[0].dtype),
            pltpu.VMEM((length, w_out.shape[1]), jnp.bfloat16),
            pltpu.SemaphoreType.DMA,
            pltpu.SemaphoreType.DMA((OUT_PARTS,)),
        ],
        compiler_params=params(40),
        cost_estimate=pl.CostEstimate(
            flops=2 * length * width * (w_out.shape[1] + 768),
            bytes_accessed=16 * length * width,
            transcendentals=length * 384 * HEADS,
        ),
        name="finish",
    )(away, projected, own_sum, top, total, reads, leads, w_out, *pages, *states)


def shifted(block, axis, distance):
    size = lax.axis_size(axis)
    return lax.ppermute(block, axis, [((i - distance) % size, i) for i in range(size)])


def exchanged(block, axis, bit):
    return lax.ppermute(block, axis, [(i ^ bit, i) for i in range(lax.axis_size(axis))])


def migrate(code, payload, beside, arrays):
    groups = lax.axis_size("req")
    orders = list(itertools.permutations(range(groups)))

    def branch(order):
        route = [(order[g], g) for g in range(groups)]
        return lambda x, *xs: (lax.ppermute(x, "req", route),) + tuple(beside(*xs))

    return lax.switch(code, [branch(order) for order in orders], payload, *arrays)


def on_device(
    tokens,
    norm_gain,
    w_qkv,
    w_out,
    w_gates,
    gate_bias,
    persistent,
    cache,
    page_back,
    page_fill,
    mem_state,
    mig_source,
):
    pages = cache.shape[2]
    rows = cache.reshape(-1, cache.shape[-1])
    payload, code, away, relay = prepare(mig_source, page_back, page_fill, rows)
    moved, projected, gates, state = migrate(
        code[0], payload, project, (tokens[0, 0], norm_gain, w_qkv, jnp.transpose(w_gates), mem_state[0, 0])
    )
    packed = pack_pages(moved, pages, cache.shape[3:])
    state, *packed = lax.optimization_barrier((state, *packed))
    near = exchanged(state, "req", 1)
    ahead = [shifted(packed[k], "seq", -k) for k in (4, 2, 3)]
    near, fifth, projected = lax.optimization_barrier((near, packed[5], projected))
    far = exchanged(jnp.where(relay[0] == 1, near, state), "req", 2)
    ahead.append(shifted(fifth, "seq", -5))
    own_sum, top, total = own_attention(projected, persistent, packed[0])
    first, _ = lax.optimization_barrier((packed[1], top))
    arrived = [shifted(first, "seq", -1)] + ahead
    reads, leads = memory_reads(projected, gates, gate_bias)
    result = finish(
        away, projected, own_sum, top, total, reads, leads, w_out, arrived, (state, near, far)
    )
    return result[None, None]


def solution(mesh):
    return jax.shard_map(
        on_device,
        mesh=mesh,
        in_specs=(
            P("req", "seq", None, None),
            P(),
            P(),
            P(),
            P(),
            P(),
            P(),
            P("req", "seq", None, None, None, None),
            P("req", "seq", None),
            P("req", "seq", None),
            P("req", "seq", None, None, None),
            P("seq", None),
        ),
        out_specs=P("req", "seq", None, None),
        check_vma=False,
    )
```
